128 devices in a mesh: dp: 16 (over z, x), ep: 8 (over y, core).
Axes of the slice: x: 4, y: 4, z: 4, core: 2. Of those that a mesh axis runs over, the one named last changes fastest.
Arguments:
- hidden: bfloat16 [2, 2048, 3584], P(None, ('dp', 'ep')), may hold values from -6 to 6
- routes: int32 [2, 2048, 8], P(None, ('dp', 'ep')), may hold values from 0 to 127, all different within a row; in each aligned block of 16 rows (0 to 15, 16 to 31, ..., all dimensions but the last counted through in order) at most 2 rows name the same one
- route_weights: float32 [2, 2048, 8], P(None, ('dp', 'ep')), may hold values from 0.1 to 0.6
- expert_in: bfloat16 [128, 3584, 2048], P(('dp', 'ep')), may hold values from -0.09375 to 0.09375
- expert_out: bfloat16 [128, 1024, 3584], P(('dp', 'ep')), may hold values from -0.1875 to 0.1875
- queries: bfloat16 [2048, 64, 576], P(('dp', 'ep')), may hold values from -6 to 6
- fresh_key: bfloat16 [2048, 576], P(('dp', 'ep')), may hold values from -4 to 4
- latent_cache: bfloat16 [2048, 128, 576], P(('dp', 'ep')), may hold values from -4 to 4
- lengths: int32 [2048], replicated, may hold values from 2 to 128, as said below
- swapped: int32 [2048], P(('dp', 'ep')), may hold values from 0 to 1, as said below
Outputs:
- mixed: bfloat16 [2, 2048, 3584], P(None, ('dp', 'ep'))
- context: bfloat16 [2048, 64, 512], P(('dp', 'ep'))
The draws below stay inside these ranges and needn't reach their ends.
Inputs may be any that keep to these rules, and one draw needn't show every extreme that they name: `routes`: in each step the 8 experts of a token differ; the 16 tokens of one device name one expert at most 2 times, a bound that some block reaches. `lengths`: some request holds exactly 128 positions. `swapped`: A marked slot trades with the slot at the same position on the device of the same ep index whose dp index differs by half the dp axis; both devices of such a pair carry the same marks; a device carries at most 4 marks, and some device exactly 4.
All inputs are finite; a program needn't handle non-finite values.
Results may differ from the reference program's by a relative error of at most 0.0058.
Values may be sent and summed in bfloat16 or wider, within the bound.
A program may use at most 128 MiB of HBM per device.

```python
import math
import jax
import jax.numpy as jnp
import numpy as np
from jax import lax

D = 3584
FF = 1024
HEADS = 64
LATENT = 512
ROPE = 64
TOPK = 8
STEPS = 2
MOVE = 4
TOK_DEV = 16
LMAX = 128
EXPERTS = 128
CAP = 2
TOKENS = 2048
N_DP = 16
N_EP = 8


def pair_mask(key):
    base = jax.random.fold_in(key, 101)
    pair_count = TOKENS // (2 * TOK_DEV)
    moving = jax.random.randint(jax.random.fold_in(base, 1), (pair_count,), 1, MOVE + 1)
    moving = moving.at[0].set(MOVE)
    ranking = jax.random.randint(jax.random.fold_in(base, 2), (pair_count, TOK_DEV), 0, 1 << 20) * TOK_DEV + jnp.arange(TOK_DEV, dtype=jnp.int32)[None, :]
    ranked = jnp.argsort(jnp.argsort(ranking, axis=1), axis=1)
    lower = (ranked < moving[:, None]).astype(jnp.int32)
    return jnp.concatenate([lower, lower], axis=0).reshape(-1)


def draw_swapped(key, part):
    return pair_mask(key).astype(jnp.int32)


def draw_lengths(key, part):
    base = jax.random.fold_in(key, 202)
    pair_count = TOKENS // (2 * TOK_DEV)
    side = jax.random.randint(jax.random.fold_in(base, 1), (pair_count,), 0, 2)
    heavy = jnp.concatenate([side, 1 - side])
    longer = jax.random.randint(jax.random.fold_in(base, 2), (2 * pair_count, TOK_DEV), LMAX // 2, LMAX + 1)
    shorter = jax.random.randint(jax.random.fold_in(base, 3), (2 * pair_count, TOK_DEV), 2, LMAX // 2 + 1)
    chosen = jnp.where(heavy[:, None] == 1, longer, shorter).reshape(-1)
    return chosen.at[0].set(LMAX).astype(jnp.int32)


def draw_latent_cache(key, part):
    full_width = LATENT + ROPE
    drawn = jax.random.normal(jax.random.fold_in(key, 405), (TOKENS, LMAX, full_width), jnp.float32)
    return jnp.clip(drawn, -4.0, 4.0).astype(jnp.bfloat16)


def draw_queries(key, part):
    full_width = LATENT + ROPE
    drawn = jax.random.normal(jax.random.fold_in(key, 508), (TOKENS, HEADS, full_width), jnp.float32)
    return jnp.clip(drawn, -4.0, 4.0).astype(jnp.bfloat16)


def block_levels(stream_key, dims, shards, low, largest):
    gain = 1.0
    for position, parts in shards:
        steps = jax.random.uniform(jax.random.fold_in(jax.random.fold_in(stream_key, 6), position), (parts,), jnp.float32, low / len(shards), largest / len(shards))
        gain = gain * jnp.repeat(jnp.exp(steps), dims[position] // parts).reshape((-1,) + (1,) * (len(dims) - 1 - position))
    return gain


def shared_out(stream_key, own, number, rows, count, top, reach, skew):
    sequence = jax.random.permutation(stream_key, count)
    crowded, common = shares(count, rows * top, reach, skew, True), shares(count, rows * top, reach, skew, False)
    places = jnp.arange(count)

    def named(sizes, rotation):
        used = int((sizes > 0).sum())
        fixed = max(1, used // 4)
        shifted = fixed + (places - fixed + rotation * (used - fixed)) % max(1, count - fixed)
        return jnp.zeros((count,), jnp.int32).at[sequence[jnp.where(places < fixed, places, shifted)]].set(jnp.asarray(sizes, jnp.int32))

    sizes = jnp.where(number % 4 == 0, named(crowded, number // 4), named(common, number - number // 4 - 1))
    mixed = jax.random.permutation(jax.random.fold_in(own, 3), count)
    source_of, taker = mixed[0:count // 2 * 2:2], mixed[1:count // 2 * 2:2]
    margin = jnp.minimum(sizes[source_of] - 1, reach - sizes[taker]) // 2
    margin = jnp.where((source_of == sequence[0]) | (taker == sequence[0]) | (sizes[taker] == 0), 0, jnp.maximum(margin, 0))
    shifted = jax.random.randint(jax.random.fold_in(own, 4), (count // 2,), 0, 1 << 20) % (margin + 1)
    sizes = sizes.at[source_of].add(-shifted).at[taker].add(shifted)
    labels = jnp.searchsorted(jnp.cumsum(sizes), jnp.arange(rows * top), side="right").astype(jnp.int32)
    listing = labels.reshape(top, rows).T
    listing = listing[jax.random.permutation(jax.random.fold_in(own, 1), rows)]
    rotation = jax.random.randint(jax.random.fold_in(own, 2), (rows, 1), 0, top)
    return jnp.take_along_axis(listing, (jnp.arange(top)[None, :] + rotation) % top, axis=1)


def shares(count, total, limit, lean, full):
    loads = [(1 << 20) // math.isqrt(standing ** lean) + 1 for standing in range(1, count + 1)]
    largest = limit if full else min(limit, max(-(-total // count), total * loads[0] // sum(loads)))
    least = 1 if total - largest >= count - 1 else 0
    counts, spare = [largest] + [least] * (count - 1), total - largest - least * (count - 1)
    while spare > 0:
        movable = [i for i in range(1, count) if counts[i] < largest] or [i for i in range(1, count) if counts[i] < limit]
        whole, budget = sum([loads[i] for i in movable]), spare
        for i in movable:
            extra = min(limit - counts[i], max(1, budget * loads[i] // whole), spare)
            counts[i] = counts[i] + extra
            spare = spare - extra
    return np.array(counts)


def centred(rng, shape, spread, reach, shards=(), kind=jnp.bfloat16):
    values = spread * jax.random.normal(rng, shape, jnp.float32)
    if shards:
        values = values * block_levels(rng, shape, shards, -0.22, 0.18)
    return jnp.clip(values, -reach, reach).astype(kind)


def setup_inputs(seed: int = 0) -> dict:
    streams_of = jax.random.split(jax.random.key(seed), 11)
    hidden = centred(streams_of[0], (STEPS, TOKENS, D), 1.0, 6.0, ((1, 128),))
    routes_keys = jax.random.split(jax.random.fold_in(streams_of[1], 1), STEPS * TOKENS // TOK_DEV)
    routes_turns = jax.random.permutation(jax.random.fold_in(streams_of[1], 3), STEPS * TOKENS // TOK_DEV)
    routes = jax.vmap(lambda own, number: shared_out(jax.random.fold_in(streams_of[1], 2), own, number, TOK_DEV, N_DP * N_EP, TOPK, CAP, 1))(routes_keys, routes_turns).reshape((STEPS, TOKENS, TOPK))
    route_weights = jnp.clip(0.1 + 0.5 * jax.random.uniform(streams_of[2], (STEPS, TOKENS, TOPK), jnp.float32) ** block_levels(streams_of[2], (STEPS, TOKENS, TOPK), ((1, 128),), -0.2, 0.2), 0.1, 0.6)
    expert_in = centred(streams_of[3], (EXPERTS, D, 2 * FF), D ** -0.5, 0.09375, ((0, 128),))
    expert_out = centred(streams_of[4], (EXPERTS, FF, D), FF ** -0.5, 0.1875, ((0, 128),))
    queries = draw_queries(jax.random.fold_in(streams_of[10], 71), 0)
    fresh_key = centred(streams_of[6], (TOKENS, LATENT + ROPE), 1.0, 4.0, ((0, 128),))
    latent_cache = draw_latent_cache(jax.random.fold_in(streams_of[10], 71), 0)
    lengths = draw_lengths(jax.random.fold_in(streams_of[10], 71), 0)
    swapped = draw_swapped(jax.random.fold_in(streams_of[10], 71), 0)
    return dict(hidden=hidden, routes=routes, route_weights=route_weights, expert_in=expert_in, expert_out=expert_out, queries=queries, fresh_key=fresh_key, latent_cache=latent_cache, lengths=lengths, swapped=swapped)


SOFTMAX_SCALE = 192.0 ** -0.5


def expert_rows(picked, expert_in, expert_out):
    projected = jnp.dot(picked, expert_in, preferred_element_type=jnp.float32)
    half_width = projected.shape[1] // 2
    activated = (jax.nn.silu(projected[:, :half_width]) * projected[:, half_width:]).astype(jnp.bfloat16)
    return jnp.dot(activated, expert_out, preferred_element_type=jnp.float32).astype(jnp.bfloat16)


def routed_step(hidden, routes, route_weights, expert_in, expert_out):
    flat_ids = routes.reshape(-1)
    gate_values = route_weights.reshape(-1)
    capacity = N_DP * N_EP * CAP

    def add_expert(summed, expert):
        matches = flat_ids == expert
        located = jnp.nonzero(matches, size=capacity, fill_value=0)[0].astype(jnp.int32)
        is_valid = jnp.arange(capacity, dtype=jnp.int32) < jnp.sum(matches.astype(jnp.int32))
        token_rows = located // TOPK
        result = expert_rows(hidden[token_rows], expert_in[expert], expert_out[expert]).astype(jnp.float32)
        gate_scale = jnp.where(is_valid, gate_values[located], 0.0)
        return summed.at[token_rows].add(result * gate_scale[:, None]), None

    initial = jnp.zeros((hidden.shape[0], hidden.shape[1]), jnp.float32)
    summed, _ = lax.scan(add_expert, initial, jnp.arange(EXPERTS, dtype=jnp.int32))
    return summed.astype(jnp.bfloat16)


def attend_request(query_rows, cache_rows, length, fresh_row):
    scores = jnp.dot(query_rows, cache_rows.T, preferred_element_type=jnp.float32) * SOFTMAX_SCALE
    own_score = jnp.dot(query_rows, fresh_row, preferred_element_type=jnp.float32) * SOFTMAX_SCALE
    live_mask = jnp.arange(cache_rows.shape[0], dtype=jnp.int32) < length
    scores = jnp.where(live_mask[None, :], scores, -jnp.inf)
    row_top = jnp.maximum(jnp.max(scores, axis=1), own_score)
    weights = jnp.exp(scores - row_top[:, None])
    own_weight = jnp.exp(own_score - row_top)
    summed = jnp.sum(weights, axis=1) + own_weight
    blended = jnp.dot(weights.astype(jnp.bfloat16), cache_rows[:, :LATENT], preferred_element_type=jnp.float32)
    own_rounded = lax.optimization_barrier(own_weight.astype(jnp.bfloat16))
    blended = blended + own_rounded.astype(jnp.float32)[:, None] * fresh_row[None, :LATENT].astype(jnp.float32)
    return (blended / summed[:, None]).astype(jnp.bfloat16)


def reference(hidden, routes, route_weights, expert_in, expert_out, queries, fresh_key, latent_cache, lengths, swapped):
    mixed = jnp.stack([routed_step(hidden[step], routes[step], route_weights[step], expert_in, expert_out) for step in range(STEPS)])
    request_ids = jnp.arange(TOKENS, dtype=jnp.int32)
    anchor = jnp.where(swapped == 1, (request_ids + TOKENS // 2) % TOKENS, request_ids).astype(jnp.int32)

    def single_request(request):
        source = anchor[request]
        return attend_request(queries[request], latent_cache[source], lengths[source], fresh_key[request])

    context = lax.map(single_request, request_ids)
    return mixed, context
```

```python
import functools

import jax
import jax.numpy as jnp
from jax import lax
from jax.experimental import pallas as pl
from jax.experimental.pallas import tpu as pltpu
from jax.sharding import PartitionSpec as P

LATENT = 512
STEPS = 2
MOVE = 4
CAP = 2
MESH_ID = pl.DeviceIdType.MESH

SOFTMAX_SCALE = 192.0 ** (-0.5)


def _a2a_kernel(n_ep, n_all, x_ref, o_ref, send_sem, recv_sem):
    me = lax.axis_index("dp") * n_ep + lax.axis_index("ep")
    barrier = pltpu.get_barrier_semaphore()

    def greet(k, carry):
        peer = lax.rem(me + k, n_all)
        pl.semaphore_signal(
            barrier, 1, device_id=(peer // n_ep, peer % n_ep), device_id_type=MESH_ID
        )
        return carry

    lax.fori_loop(1, n_all, greet, 0)
    pl.semaphore_wait(barrier, n_all - 1)
    pltpu.make_async_copy(x_ref.at[me], o_ref.at[me], recv_sem).start()

    def send(k, carry):
        peer = lax.rem(me + k, n_all)
        pltpu.make_async_remote_copy(
            x_ref.at[peer],
            o_ref.at[me],
            send_sem,
            recv_sem,
            device_id=(peer // n_ep, peer % n_ep),
            device_id_type=MESH_ID,
        ).start()
        return carry

    lax.fori_loop(1, n_all, send, 0)
    sent = pl.ds(0, n_all - 1)
    pltpu.make_async_copy(x_ref.at[sent], x_ref.at[sent], send_sem).wait()
    pltpu.make_async_copy(o_ref, o_ref, recv_sem).wait()


def all_to_all_rows(x, n_ep, n_all, collective_id):
    nbytes = x.size * x.dtype.itemsize
    return pl.pallas_call(
        functools.partial(_a2a_kernel, n_ep, n_all),
        out_shape=jax.ShapeDtypeStruct(x.shape, x.dtype),
        in_specs=[pl.BlockSpec(memory_space=pl.ANY)],
        out_specs=pl.BlockSpec(memory_space=pl.ANY),
        scratch_shapes=[pltpu.SemaphoreType.DMA(()), pltpu.SemaphoreType.DMA(())],
        compiler_params=pltpu.CompilerParams(collective_id=collective_id, has_side_effects=True),
        cost_estimate=pl.CostEstimate(flops=0, transcendentals=0, bytes_accessed=2 * nbytes),
    )(x)


def swapped_2(value, axis, apart):
    mask = 2**apart
    pairs = [(source, source ^ mask) for source in range(lax.axis_size(axis))]
    return lax.ppermute(value, axis, pairs)


def expert_rows(picked, expert_in, expert_out):
    projected = jnp.einsum("skc,cf->skf", picked, expert_in, preferred_element_type=jnp.float32)
    half_width = projected.shape[2] // 2
    activated = (
        jax.nn.silu(projected[:, :, :half_width]) * projected[:, :, half_width:]
    ).astype(jnp.bfloat16)
    return jnp.einsum(
        "skf,fc->skc", activated, expert_out, preferred_element_type=jnp.float32
    ).astype(jnp.bfloat16)


def pack_rows(tokens, experts, expert_count, slot_cap):
    step_count, token_count, pick_count = experts.shape
    onehot = (experts[:, :, :, None] == jnp.arange(expert_count, dtype=jnp.int32)).astype(
        jnp.int32
    )
    flat = onehot.reshape(step_count, token_count * pick_count, expert_count)
    earlier = jnp.cumsum(flat, axis=1) - flat
    within = jnp.sum(earlier * flat, axis=2).reshape(step_count, token_count, pick_count)
    steps = jnp.arange(step_count, dtype=jnp.int32)[:, None, None]
    target = experts * (step_count * slot_cap) + steps * slot_cap + within
    places = jnp.arange(expert_count * step_count * slot_cap, dtype=jnp.int32).reshape(
        expert_count, step_count * slot_cap
    )
    flat_target = target.reshape(step_count * token_count, pick_count)
    select = jnp.any(flat_target[None, None, :, :] == places[:, :, None, None], axis=3).astype(
        jnp.bfloat16
    )
    flat_tokens = tokens.reshape(step_count * token_count, tokens.shape[2])
    packed = jnp.einsum(
        "dkt,tc->dkc", select, flat_tokens, preferred_element_type=jnp.float32
    ).astype(jnp.bfloat16)
    return packed, target


def unpack_rows(returned, target, gate_values):
    width = returned.shape[1]
    flat_target = target.reshape(-1)
    picked = returned[flat_target // width, flat_target % width].reshape(
        target.shape + (returned.shape[2],)
    )
    summed = jnp.sum(picked.astype(jnp.float32) * gate_values[..., None], axis=2)
    return summed.astype(jnp.bfloat16)


def attend_block(query_rows, cache_rows, live_lengths, fresh_rows):
    scores = (
        jnp.einsum("nhc,nlc->nhl", query_rows, cache_rows, preferred_element_type=jnp.float32)
        * SOFTMAX_SCALE
    )
    own_score = (
        jnp.einsum("nhc,nc->nh", query_rows, fresh_rows, preferred_element_type=jnp.float32)
        * SOFTMAX_SCALE
    )
    positions = jnp.arange(cache_rows.shape[1], dtype=jnp.int32)
    scores = jnp.where(positions[None, None, :] < live_lengths[:, None, None], scores, -jnp.inf)
    row_top = jnp.maximum(jnp.max(scores, axis=2), own_score)
    weights = jnp.exp(scores - row_top[:, :, None])
    own_weight = jnp.exp(own_score - row_top)
    summed = jnp.sum(weights, axis=2) + own_weight
    blended = jnp.einsum(
        "nhl,nlc->nhc",
        weights.astype(jnp.bfloat16),
        cache_rows[:, :, :LATENT],
        preferred_element_type=jnp.float32,
    )
    own_rounded = lax.optimization_barrier(own_weight.astype(jnp.bfloat16))
    blended = blended + own_rounded.astype(jnp.float32)[:, :, None] * fresh_rows[
        :, None, :LATENT
    ].astype(jnp.float32)
    return (blended / summed[:, :, None]).astype(jnp.bfloat16)


def per_device(
    hidden,
    routes,
    route_weights,
    expert_in,
    expert_out,
    queries,
    fresh_key,
    latent_cache,
    lengths,
    swapped,
):
    n_ep = lax.axis_size("ep")
    expert_count = lax.axis_size("dp") * n_ep
    packed, target = pack_rows(hidden, routes, expert_count, CAP)
    received = all_to_all_rows(packed, n_ep, expert_count, 0)
    finished = expert_rows(received, expert_in[0], expert_out[0])
    returned = all_to_all_rows(finished, n_ep, expert_count, 1)
    mixed = unpack_rows(returned, target, route_weights)
    row_count = swapped.shape[0]
    top_bit = lax.axis_size("dp").bit_length() - 2
    outgoing = jnp.argsort(1 - swapped, stable=True)[:MOVE]
    arrival = jnp.clip(jnp.cumsum(swapped) - 1, 0, MOVE - 1)
    is_moved = swapped == 1
    device_rows = lax.axis_index(("dp", "ep")) * row_count + jnp.arange(row_count, dtype=jnp.int32)
    total_rows = expert_count * row_count
    anchor = jnp.where(is_moved, (device_rows + total_rows // 2) % total_rows, device_rows)
    incoming_cache = swapped_2(latent_cache[outgoing], "dp", top_bit)
    merged_cache = jnp.where(is_moved[:, None, None], incoming_cache[arrival], latent_cache)
    context = attend_block(queries, merged_cache, lengths[anchor], fresh_key)
    return (mixed, context)


def solution(mesh):
    in_specs = (
        P(None, ("dp", "ep"), None),
        P(None, ("dp", "ep"), None),
        P(None, ("dp", "ep"), None),
        P(("dp", "ep"), None, None),
        P(("dp", "ep"), None, None),
        P(("dp", "ep"), None, None),
        P(("dp", "ep"), None),
        P(("dp", "ep"), None, None),
        P(),
        P(("dp", "ep")),
    )
    out_specs = (P(None, ("dp", "ep"), None), P(("dp", "ep"), None, None))
    return jax.shard_map(
        per_device, mesh=mesh, in_specs=in_specs, out_specs=out_specs, check_vma=False
    )
```

```python
import functools

import jax
import jax.numpy as jnp
from jax import lax
from jax.experimental import pallas as pl
from jax.experimental.pallas import tpu as pltpu
from jax.sharding import PartitionSpec as P

LATENT = 512
STEPS = 2
MOVE = 4
CAP = 2
MESH_ID = pl.DeviceIdType.MESH

SOFTMAX_SCALE = 192.0 ** (-0.5)


def _a2a_kernel(n_ep, n_all, x_ref, o_ref, send_sem, recv_sem):
    me = lax.axis_index("dp") * n_ep + lax.axis_index("ep")
    barrier = pltpu.get_barrier_semaphore()

    def greet(k, carry):
        peer = lax.rem(me + k, n_all)
        pl.semaphore_signal(
            barrier, 1, device_id=(peer // n_ep, peer % n_ep), device_id_type=MESH_ID
        )
        return carry

    lax.fori_loop(1, n_all, greet, 0)
    pl.semaphore_wait(barrier, n_all - 1)
    pltpu.make_async_copy(x_ref.at[me], o_ref.at[me], recv_sem).start()

    def send(k, carry):
        peer = lax.rem(me + k, n_all)
        pltpu.make_async_remote_copy(
            x_ref.at[peer],
            o_ref.at[me],
            send_sem,
            recv_sem,
            device_id=(peer // n_ep, peer % n_ep),
            device_id_type=MESH_ID,
        ).start()
        return carry

    lax.fori_loop(1, n_all, send, 0)
    sent = pl.ds(0, n_all - 1)
    pltpu.make_async_copy(x_ref.at[sent], x_ref.at[sent], send_sem).wait()
    pltpu.make_async_copy(o_ref, o_ref, recv_sem).wait()


def all_to_all_rows(x, n_ep, n_all, collective_id):
    nbytes = x.size * x.dtype.itemsize
    return pl.pallas_call(
        functools.partial(_a2a_kernel, n_ep, n_all),
        out_shape=jax.ShapeDtypeStruct(x.shape, x.dtype),
        in_specs=[pl.BlockSpec(memory_space=pl.ANY)],
        out_specs=pl.BlockSpec(memory_space=pl.ANY),
        scratch_shapes=[pltpu.SemaphoreType.DMA(()), pltpu.SemaphoreType.DMA(())],
        compiler_params=pltpu.CompilerParams(collective_id=collective_id, has_side_effects=True),
        cost_estimate=pl.CostEstimate(flops=0, transcendentals=0, bytes_accessed=2 * nbytes),
    )(x)


def swapped_2(value, axis, apart):
    mask = 2**apart
    pairs = [(source, source ^ mask) for source in range(lax.axis_size(axis))]
    return lax.ppermute(value, axis, pairs)


def expert_rows(picked, expert_in, expert_out):
    projected = jnp.einsum("skc,cf->skf", picked, expert_in, preferred_element_type=jnp.float32)
    half_width = projected.shape[2] // 2
    activated = (
        jax.nn.silu(projected[:, :, :half_width]) * projected[:, :, half_width:]
    ).astype(jnp.bfloat16)
    return jnp.einsum(
        "skf,fc->skc", activated, expert_out, preferred_element_type=jnp.float32
    ).astype(jnp.bfloat16)


def pack_rows(tokens, experts, expert_count, slot_cap):
    step_count, token_count, pick_count = experts.shape
    onehot = (experts[:, :, :, None] == jnp.arange(expert_count, dtype=jnp.int32)).astype(
        jnp.int32
    )
    flat = onehot.reshape(step_count, token_count * pick_count, expert_count)
    earlier = jnp.cumsum(flat, axis=1) - flat
    within = jnp.sum(earlier * flat, axis=2).reshape(step_count, token_count, pick_count)
    steps = jnp.arange(step_count, dtype=jnp.int32)[:, None, None]
    target = experts * (step_count * slot_cap) + steps * slot_cap + within
    places = jnp.arange(expert_count * step_count * slot_cap, dtype=jnp.int32).reshape(
        expert_count, step_count * slot_cap
    )
    flat_target = target.reshape(step_count * token_count, pick_count)
    select = jnp.any(flat_target[None, None, :, :] == places[:, :, None, None], axis=3).astype(
        jnp.bfloat16
    )
    flat_tokens = tokens.reshape(step_count * token_count, tokens.shape[2])
    packed = jnp.einsum(
        "dkt,tc->dkc", select, flat_tokens, preferred_element_type=jnp.float32
    ).astype(jnp.bfloat16)
    return packed, target


def unpack_rows(returned, target, gate_values):
    width = returned.shape[1]
    flat_target = target.reshape(-1)
    picked = returned[flat_target // width, flat_target % width].reshape(
        target.shape + (returned.shape[2],)
    )
    summed = jnp.sum(picked.astype(jnp.float32) * gate_values[..., None], axis=2)
    return summed.astype(jnp.bfloat16)


def attend_block(query_rows, cache_rows, live_lengths, fresh_rows):
    scores = (
        jnp.einsum("nhc,nlc->nhl", query_rows, cache_rows, preferred_element_type=jnp.float32)
        * SOFTMAX_SCALE
    )
    own_score = (
        jnp.einsum("nhc,nc->nh", query_rows, fresh_rows, preferred_element_type=jnp.float32)
        * SOFTMAX_SCALE
    )
    positions = jnp.arange(cache_rows.shape[1], dtype=jnp.int32)
    scores = jnp.where(positions[None, None, :] < live_lengths[:, None, None], scores, -jnp.inf)
    row_top = jnp.maximum(jnp.max(scores, axis=2), own_score)
    weights = jnp.exp(scores - row_top[:, :, None])
    own_weight = jnp.exp(own_score - row_top)
    summed = jnp.sum(weights, axis=2) + own_weight
    blended = jnp.einsum(
        "nhl,nlc->nhc",
        weights.astype(jnp.bfloat16),
        cache_rows[:, :, :LATENT],
        preferred_element_type=jnp.float32,
    )
    own_rounded = lax.optimization_barrier(own_weight.astype(jnp.bfloat16))
    blended = blended + own_rounded.astype(jnp.float32)[:, :, None] * fresh_rows[
        :, None, :LATENT
    ].astype(jnp.float32)
    return (blended / summed[:, :, None]).astype(jnp.bfloat16)


def per_device(
    hidden,
    routes,
    route_weights,
    expert_in,
    expert_out,
    queries,
    fresh_key,
    latent_cache,
    lengths,
    swapped,
):
    n_ep = lax.axis_size("ep")
    expert_count = lax.axis_size("dp") * n_ep
    packs = [
        pack_rows(hidden[step : step + 1], routes[step : step + 1], expert_count, CAP)
        for step in range(STEPS)
    ]
    received = [lax.all_to_all(p[0], ("dp", "ep"), 0, 0, tiled=True) for p in packs]
    finished = [expert_rows(r, expert_in[0], expert_out[0]) for r in received]
    returned = [lax.all_to_all(f, ("dp", "ep"), 0, 0, tiled=True) for f in finished]
    mixed = jnp.concatenate(
        [unpack_rows(returned[step], packs[step][1], route_weights[step : step + 1]) for step in range(STEPS)]
    )
    row_count = swapped.shape[0]
    top_bit = lax.axis_size("dp").bit_length() - 2
    outgoing = jnp.argsort(1 - swapped, stable=True)[:MOVE]
    arrival = jnp.clip(jnp.cumsum(swapped) - 1, 0, MOVE - 1)
    is_moved = swapped == 1
    device_rows = lax.axis_index(("dp", "ep")) * row_count + jnp.arange(row_count, dtype=jnp.int32)
    total_rows = expert_count * row_count
    anchor = jnp.where(is_moved, (device_rows + total_rows // 2) % total_rows, device_rows)
    incoming_cache = swapped_2(latent_cache[outgoing], "dp", top_bit)
    merged_cache = jnp.where(is_moved[:, None, None], incoming_cache[arrival], latent_cache)
    context = attend_block(queries, merged_cache, lengths[anchor], fresh_key)
    return (mixed, context)


def solution(mesh):
    in_specs = (
        P(None, ("dp", "ep"), None),
        P(None, ("dp", "ep"), None),
        P(None, ("dp", "ep"), None),
        P(("dp", "ep"), None, None),
        P(("dp", "ep"), None, None),
        P(("dp", "ep"), None, None),
        P(("dp", "ep"), None),
        P(("dp", "ep"), None, None),
        P(),
        P(("dp", "ep")),
    )
    out_specs = (P(None, ("dp", "ep"), None), P(("dp", "ep"), None, None))
    return jax.shard_map(
        per_device, mesh=mesh, in_specs=in_specs, out_specs=out_specs, check_vma=False
    )
```

```python
import functools

import jax
import jax.numpy as jnp
from jax import lax
from jax.experimental import pallas as pl
from jax.experimental.pallas import tpu as pltpu
from jax.sharding import PartitionSpec as P

LATENT = 512
STEPS = 2
MOVE = 4
CAP = 2
MESH_ID = pl.DeviceIdType.MESH

SOFTMAX_SCALE = 192.0 ** (-0.5)


def _a2a_kernel(n_ep, n_all, x_ref, o_ref, send_sem, recv_sem):
    me = lax.axis_index("dp") * n_ep + lax.axis_index("ep")
    barrier = pltpu.get_barrier_semaphore()

    def greet(k, carry):
        peer = lax.rem(me + k, n_all)
        pl.semaphore_signal(
            barrier, 1, device_id=(peer // n_ep, peer % n_ep), device_id_type=MESH_ID
        )
        return carry

    lax.fori_loop(1, n_all, greet, 0)
    pl.semaphore_wait(barrier, n_all - 1)
    pltpu.make_async_copy(x_ref.at[me], o_ref.at[me], recv_sem).start()

    def send(k, carry):
        peer = lax.rem(me + k, n_all)
        pltpu.make_async_remote_copy(
            x_ref.at[peer],
            o_ref.at[me],
            send_sem,
            recv_sem,
            device_id=(peer // n_ep, peer % n_ep),
            device_id_type=MESH_ID,
        ).start()
        return carry

    lax.fori_loop(1, n_all, send, 0)
    sent = pl.ds(0, n_all - 1)
    pltpu.make_async_copy(x_ref.at[sent], x_ref.at[sent], send_sem).wait()
    pltpu.make_async_copy(o_ref, o_ref, recv_sem).wait()


def all_to_all_rows(x, n_ep, n_all, collective_id):
    nbytes = x.size * x.dtype.itemsize
    return pl.pallas_call(
        functools.partial(_a2a_kernel, n_ep, n_all),
        out_shape=jax.ShapeDtypeStruct(x.shape, x.dtype),
        in_specs=[pl.BlockSpec(memory_space=pl.ANY)],
        out_specs=pl.BlockSpec(memory_space=pl.ANY),
        scratch_shapes=[pltpu.SemaphoreType.DMA(()), pltpu.SemaphoreType.DMA(())],
        compiler_params=pltpu.CompilerParams(collective_id=collective_id, has_side_effects=True),
        cost_estimate=pl.CostEstimate(flops=0, transcendentals=0, bytes_accessed=2 * nbytes),
    )(x)


def swapped_2(value, axis, apart):
    mask = 2**apart
    pairs = [(source, source ^ mask) for source in range(lax.axis_size(axis))]
    return lax.ppermute(value, axis, pairs)


def expert_rows(picked, expert_in, expert_out):
    projected = jnp.einsum("skc,cf->skf", picked, expert_in, preferred_element_type=jnp.float32)
    half_width = projected.shape[2] // 2
    activated = (
        jax.nn.silu(projected[:, :, :half_width]) * projected[:, :, half_width:]
    ).astype(jnp.bfloat16)
    return jnp.einsum(
        "skf,fc->skc", activated, expert_out, preferred_element_type=jnp.float32
    ).astype(jnp.bfloat16)


def pack_rows(tokens, experts, expert_count, slot_cap):
    step_count, token_count, pick_count = experts.shape
    onehot = (experts[:, :, :, None] == jnp.arange(expert_count, dtype=jnp.int32)).astype(
        jnp.int32
    )
    flat = onehot.reshape(step_count, token_count * pick_count, expert_count)
    earlier = jnp.cumsum(flat, axis=1) - flat
    within = jnp.sum(earlier * flat, axis=2).reshape(step_count, token_count, pick_count)
    steps = jnp.arange(step_count, dtype=jnp.int32)[:, None, None]
    target = experts * (step_count * slot_cap) + steps * slot_cap + within
    places = jnp.arange(expert_count * step_count * slot_cap, dtype=jnp.int32).reshape(
        expert_count, step_count * slot_cap
    )
    flat_target = target.reshape(step_count * token_count, pick_count)
    select = jnp.any(flat_target[None, None, :, :] == places[:, :, None, None], axis=3).astype(
        jnp.bfloat16
    )
    flat_tokens = tokens.reshape(step_count * token_count, tokens.shape[2])
    packed = jnp.einsum(
        "dkt,tc->dkc", select, flat_tokens, preferred_element_type=jnp.float32
    ).astype(jnp.bfloat16)
    return packed, target


def unpack_rows(returned, target, gate_values):
    width = returned.shape[1]
    flat_target = target.reshape(-1)
    picked = returned[flat_target // width, flat_target % width].reshape(
        target.shape + (returned.shape[2],)
    )
    summed = jnp.sum(picked.astype(jnp.float32) * gate_values[..., None], axis=2)
    return summed.astype(jnp.bfloat16)


def attend_block(query_rows, cache_rows, live_lengths, fresh_rows):
    scores = (
        jnp.einsum("nhc,nlc->nhl", query_rows, cache_rows, preferred_element_type=jnp.float32)
        * SOFTMAX_SCALE
    )
    own_score = (
        jnp.einsum("nhc,nc->nh", query_rows, fresh_rows, preferred_element_type=jnp.float32)
        * SOFTMAX_SCALE
    )
    positions = jnp.arange(cache_rows.shape[1], dtype=jnp.int32)
    scores = jnp.where(positions[None, None, :] < live_lengths[:, None, None], scores, -jnp.inf)
    row_top = jnp.maximum(jnp.max(scores, axis=2), own_score)
    weights = jnp.exp(scores - row_top[:, :, None])
    own_weight = jnp.exp(own_score - row_top)
    summed = jnp.sum(weights, axis=2) + own_weight
    blended = jnp.einsum(
        "nhl,nlc->nhc",
        weights.astype(jnp.bfloat16),
        cache_rows[:, :, :LATENT],
        preferred_element_type=jnp.float32,
    )
    own_rounded = lax.optimization_barrier(own_weight.astype(jnp.bfloat16))
    blended = blended + own_rounded.astype(jnp.float32)[:, :, None] * fresh_rows[
        :, None, :LATENT
    ].astype(jnp.float32)
    return (blended / summed[:, :, None]).astype(jnp.bfloat16)


def per_device(
    hidden,
    routes,
    route_weights,
    expert_in,
    expert_out,
    queries,
    fresh_key,
    latent_cache,
    lengths,
    swapped,
):
    n_ep = lax.axis_size("ep")
    expert_count = lax.axis_size("dp") * n_ep
    packs = [
        pack_rows(hidden[step : step + 1], routes[step : step + 1], expert_count, CAP)
        for step in range(STEPS)
    ]
    received = [lax.all_to_all(p[0], ("dp", "ep"), 0, 0, tiled=True) for p in packs]
    received[0], queries, fresh_key, latent_cache, swapped = lax.optimization_barrier(
        (received[0], queries, fresh_key, latent_cache, swapped)
    )
    finished = [expert_rows(r, expert_in[0], expert_out[0]) for r in received]
    returned = [lax.all_to_all(f, ("dp", "ep"), 0, 0, tiled=True) for f in finished]
    mixed = jnp.concatenate(
        [unpack_rows(returned[step], packs[step][1], route_weights[step : step + 1]) for step in range(STEPS)]
    )
    row_count = swapped.shape[0]
    top_bit = lax.axis_size("dp").bit_length() - 2
    outgoing = jnp.argsort(1 - swapped, stable=True)[:MOVE]
    arrival = jnp.clip(jnp.cumsum(swapped) - 1, 0, MOVE - 1)
    is_moved = swapped == 1
    device_rows = lax.axis_index(("dp", "ep")) * row_count + jnp.arange(row_count, dtype=jnp.int32)
    total_rows = expert_count * row_count
    anchor = jnp.where(is_moved, (device_rows + total_rows // 2) % total_rows, device_rows)
    incoming_cache = swapped_2(latent_cache[outgoing], "dp", top_bit)
    merged_cache = jnp.where(is_moved[:, None, None], incoming_cache[arrival], latent_cache)
    context = attend_block(queries, merged_cache, lengths[anchor], fresh_key)
    return (mixed, context)


def solution(mesh):
    in_specs = (
        P(None, ("dp", "ep"), None),
        P(None, ("dp", "ep"), None),
        P(None, ("dp", "ep"), None),
        P(("dp", "ep"), None, None),
        P(("dp", "ep"), None, None),
        P(("dp", "ep"), None, None),
        P(("dp", "ep"), None),
        P(("dp", "ep"), None, None),
        P(),
        P(("dp", "ep")),
    )
    out_specs = (P(None, ("dp", "ep"), None), P(("dp", "ep"), None, None))
    return jax.shard_map(
        per_device, mesh=mesh, in_specs=in_specs, out_specs=out_specs, check_vma=False
    )
```

```python
import functools

import jax
import jax.numpy as jnp
from jax import lax
from jax.experimental import pallas as pl
from jax.experimental.pallas import tpu as pltpu
from jax.sharding import PartitionSpec as P

LATENT = 512
STEPS = 2
MOVE = 4
CAP = 2
MESH_ID = pl.DeviceIdType.MESH

SOFTMAX_SCALE = 192.0 ** (-0.5)


def _a2a_kernel(n_ep, n_all, x_ref, o_ref, send_sem, recv_sem):
    me = lax.axis_index("dp") * n_ep + lax.axis_index("ep")
    barrier = pltpu.get_barrier_semaphore()

    def greet(k, carry):
        peer = lax.rem(me + k, n_all)
        pl.semaphore_signal(
            barrier, 1, device_id=(peer // n_ep, peer % n_ep), device_id_type=MESH_ID
        )
        return carry

    lax.fori_loop(1, n_all, greet, 0)
    pl.semaphore_wait(barrier, n_all - 1)
    pltpu.make_async_copy(x_ref.at[me], o_ref.at[me], recv_sem).start()

    def send(k, carry):
        peer = lax.rem(me + k, n_all)
        pltpu.make_async_remote_copy(
            x_ref.at[peer],
            o_ref.at[me],
            send_sem,
            recv_sem,
            device_id=(peer // n_ep, peer % n_ep),
            device_id_type=MESH_ID,
        ).start()
        return carry

    lax.fori_loop(1, n_all, send, 0)
    sent = pl.ds(0, n_all - 1)
    pltpu.make_async_copy(x_ref.at[sent], x_ref.at[sent], send_sem).wait()
    pltpu.make_async_copy(o_ref, o_ref, recv_sem).wait()


def all_to_all_rows(x, n_ep, n_all, collective_id):
    nbytes = x.size * x.dtype.itemsize
    return pl.pallas_call(
        functools.partial(_a2a_kernel, n_ep, n_all),
        out_shape=jax.ShapeDtypeStruct(x.shape, x.dtype),
        in_specs=[pl.BlockSpec(memory_space=pl.ANY)],
        out_specs=pl.BlockSpec(memory_space=pl.ANY),
        scratch_shapes=[pltpu.SemaphoreType.DMA(()), pltpu.SemaphoreType.DMA(())],
        compiler_params=pltpu.CompilerParams(collective_id=collective_id, has_side_effects=True),
        cost_estimate=pl.CostEstimate(flops=0, transcendentals=0, bytes_accessed=2 * nbytes),
    )(x)


def swapped_2(value, axis, apart):
    mask = 2**apart
    pairs = [(source, source ^ mask) for source in range(lax.axis_size(axis))]
    return lax.ppermute(value, axis, pairs)


def expert_rows(picked, expert_in, expert_out):
    projected = jnp.einsum("skc,cf->skf", picked, expert_in, preferred_element_type=jnp.float32)
    half_width = projected.shape[2] // 2
    activated = (
        jax.nn.silu(projected[:, :, :half_width]) * projected[:, :, half_width:]
    ).astype(jnp.bfloat16)
    return jnp.einsum(
        "skf,fc->skc", activated, expert_out, preferred_element_type=jnp.float32
    ).astype(jnp.bfloat16)


def pack_rows(tokens, experts, expert_count, slot_cap):
    step_count, token_count, pick_count = experts.shape
    onehot = (experts[:, :, :, None] == jnp.arange(expert_count, dtype=jnp.int32)).astype(
        jnp.int32
    )
    flat = onehot.reshape(step_count, token_count * pick_count, expert_count)
    earlier = jnp.cumsum(flat, axis=1) - flat
    within = jnp.sum(earlier * flat, axis=2).reshape(step_count, token_count, pick_count)
    steps = jnp.arange(step_count, dtype=jnp.int32)[:, None, None]
    target = experts * (step_count * slot_cap) + steps * slot_cap + within
    places = jnp.arange(expert_count * step_count * slot_cap, dtype=jnp.int32).reshape(
        expert_count, step_count * slot_cap
    )
    flat_target = target.reshape(step_count * token_count, pick_count)
    select = jnp.any(flat_target[None, None, :, :] == places[:, :, None, None], axis=3).astype(
        jnp.bfloat16
    )
    flat_tokens = tokens.reshape(step_count * token_count, tokens.shape[2])
    packed = jnp.einsum(
        "dkt,tc->dkc", select, flat_tokens, preferred_element_type=jnp.float32
    ).astype(jnp.bfloat16)
    return packed, target


def unpack_rows(returned, target, gate_values):
    width = returned.shape[1]
    flat_target = target.reshape(-1)
    picked = returned[flat_target // width, flat_target % width].reshape(
        target.shape + (returned.shape[2],)
    )
    summed = jnp.sum(picked.astype(jnp.float32) * gate_values[..., None], axis=2)
    return summed.astype(jnp.bfloat16)


def attend_block(query_rows, cache_rows, live_lengths, fresh_rows):
    scores = (
        jnp.einsum("nhc,nlc->nhl", query_rows, cache_rows, preferred_element_type=jnp.float32)
        * SOFTMAX_SCALE
    )
    own_score = (
        jnp.einsum("nhc,nc->nh", query_rows, fresh_rows, preferred_element_type=jnp.float32)
        * SOFTMAX_SCALE
    )
    positions = jnp.arange(cache_rows.shape[1], dtype=jnp.int32)
    scores = jnp.where(positions[None, None, :] < live_lengths[:, None, None], scores, -jnp.inf)
    row_top = jnp.maximum(jnp.max(scores, axis=2), own_score)
    weights = jnp.exp(scores - row_top[:, :, None])
    own_weight = jnp.exp(own_score - row_top)
    summed = jnp.sum(weights, axis=2) + own_weight
    blended = jnp.einsum(
        "nhl,nlc->nhc",
        weights.astype(jnp.bfloat16),
        cache_rows[:, :, :LATENT],
        preferred_element_type=jnp.float32,
    )
    own_rounded = lax.optimization_barrier(own_weight.astype(jnp.bfloat16))
    blended = blended + own_rounded.astype(jnp.float32)[:, :, None] * fresh_rows[
        :, None, :LATENT
    ].astype(jnp.float32)
    return (blended / summed[:, :, None]).astype(jnp.bfloat16)


def per_device(
    hidden,
    routes,
    route_weights,
    expert_in,
    expert_out,
    queries,
    fresh_key,
    latent_cache,
    lengths,
    swapped,
):
    n_ep = lax.axis_size("ep")
    expert_count = lax.axis_size("dp") * n_ep
    packed, target = pack_rows(hidden, routes, expert_count, CAP)
    received = lax.all_to_all(packed, ("dp", "ep"), 0, 0, tiled=True)
    finished = expert_rows(received, expert_in[0], expert_out[0])
    returned = lax.all_to_all(finished, ("dp", "ep"), 0, 0, tiled=True)
    mixed = unpack_rows(returned, target, route_weights)
    row_count = swapped.shape[0]
    top_bit = lax.axis_size("dp").bit_length() - 2
    outgoing = jnp.argsort(1 - swapped, stable=True)[:MOVE]
    arrival = jnp.clip(jnp.cumsum(swapped) - 1, 0, MOVE - 1)
    is_moved = swapped == 1
    device_rows = lax.axis_index(("dp", "ep")) * row_count + jnp.arange(row_count, dtype=jnp.int32)
    total_rows = expert_count * row_count
    anchor = jnp.where(is_moved, (device_rows + total_rows // 2) % total_rows, device_rows)
    incoming_cache = swapped_2(latent_cache[outgoing], "dp", top_bit)
    merged_cache = jnp.where(is_moved[:, None, None], incoming_cache[arrival], latent_cache)
    context = attend_block(queries, merged_cache, lengths[anchor], fresh_key)
    return (mixed, context)


def solution(mesh):
    in_specs = (
        P(None, ("dp", "ep"), None),
        P(None, ("dp", "ep"), None),
        P(None, ("dp", "ep"), None),
        P(("dp", "ep"), None, None),
        P(("dp", "ep"), None, None),
        P(("dp", "ep"), None, None),
        P(("dp", "ep"), None),
        P(("dp", "ep"), None, None),
        P(),
        P(("dp", "ep")),
    )
    out_specs = (P(None, ("dp", "ep"), None), P(("dp", "ep"), None, None))
    return jax.shard_map(
        per_device, mesh=mesh, in_specs=in_specs, out_specs=out_specs, check_vma=False
    )
```

```python
import functools

import jax
import jax.numpy as jnp
from jax import lax
from jax.experimental import pallas as pl
from jax.experimental.pallas import tpu as pltpu
from jax.sharding import PartitionSpec as P

LATENT = 512
STEPS = 2
MOVE = 4
CAP = 2
MESH_ID = pl.DeviceIdType.MESH

SOFTMAX_SCALE = 192.0 ** (-0.5)


def _a2a_kernel(n_ep, n_all, x_ref, o_ref, send_sem, recv_sem):
    me = lax.axis_index("dp") * n_ep + lax.axis_index("ep")
    barrier = pltpu.get_barrier_semaphore()

    def greet(k, carry):
        peer = lax.rem(me + k, n_all)
        pl.semaphore_signal(
            barrier, 1, device_id=(peer // n_ep, peer % n_ep), device_id_type=MESH_ID
        )
        return carry

    lax.fori_loop(1, n_all, greet, 0)
    pl.semaphore_wait(barrier, n_all - 1)
    pltpu.make_async_copy(x_ref.at[me], o_ref.at[me], recv_sem).start()

    def send(k, carry):
        peer = lax.rem(me + k, n_all)
        pltpu.make_async_remote_copy(
            x_ref.at[peer],
            o_ref.at[me],
            send_sem,
            recv_sem,
            device_id=(peer // n_ep, peer % n_ep),
            device_id_type=MESH_ID,
        ).start()
        return carry

    lax.fori_loop(1, n_all, send, 0)
    sent = pl.ds(0, n_all - 1)
    pltpu.make_async_copy(x_ref.at[sent], x_ref.at[sent], send_sem).wait()
    pltpu.make_async_copy(o_ref, o_ref, recv_sem).wait()


def all_to_all_rows(x, n_ep, n_all, collective_id):
    nbytes = x.size * x.dtype.itemsize
    return pl.pallas_call(
        functools.partial(_a2a_kernel, n_ep, n_all),
        out_shape=jax.ShapeDtypeStruct(x.shape, x.dtype),
        in_specs=[pl.BlockSpec(memory_space=pl.ANY)],
        out_specs=pl.BlockSpec(memory_space=pl.ANY),
        scratch_shapes=[pltpu.SemaphoreType.DMA(()), pltpu.SemaphoreType.DMA(())],
        compiler_params=pltpu.CompilerParams(collective_id=collective_id, has_side_effects=True),
        cost_estimate=pl.CostEstimate(flops=0, transcendentals=0, bytes_accessed=2 * nbytes),
    )(x)


def swapped_2(value, axis, apart):
    mask = 2**apart
    pairs = [(source, source ^ mask) for source in range(lax.axis_size(axis))]
    return lax.ppermute(value, axis, pairs)


def expert_rows(picked, expert_in, expert_out):
    projected = jnp.einsum("skc,cf->skf", picked, expert_in, preferred_element_type=jnp.float32)
    half_width = projected.shape[2] // 2
    activated = (
        jax.nn.silu(projected[:, :, :half_width]) * projected[:, :, half_width:]
    ).astype(jnp.bfloat16)
    return jnp.einsum(
        "skf,fc->skc", activated, expert_out, preferred_element_type=jnp.float32
    ).astype(jnp.bfloat16)


def pack_rows(tokens, experts, expert_count, slot_cap):
    step_count, token_count, pick_count = experts.shape
    onehot = (experts[:, :, :, None] == jnp.arange(expert_count, dtype=jnp.int32)).astype(
        jnp.int32
    )
    flat = onehot.reshape(step_count, token_count * pick_count, expert_count)
    earlier = jnp.cumsum(flat, axis=1) - flat
    within = jnp.sum(earlier * flat, axis=2).reshape(step_count, token_count, pick_count)
    steps = jnp.arange(step_count, dtype=jnp.int32)[:, None, None]
    target = experts * (step_count * slot_cap) + steps * slot_cap + within
    places = jnp.arange(expert_count * step_count * slot_cap, dtype=jnp.int32).reshape(
        expert_count, step_count * slot_cap
    )
    flat_target = target.reshape(step_count * token_count, pick_count)
    select = jnp.any(flat_target[None, None, :, :] == places[:, :, None, None], axis=3).astype(
        jnp.bfloat16
    )
    flat_tokens = tokens.reshape(step_count * token_count, tokens.shape[2])
    packed = jnp.einsum(
        "dkt,tc->dkc", select, flat_tokens, preferred_element_type=jnp.float32
    ).astype(jnp.bfloat16)
    return packed, target


def unpack_rows(returned, target, gate_values):
    width = returned.shape[1]
    flat_target = target.reshape(-1)
    picked = returned[flat_target // width, flat_target % width].reshape(
        target.shape + (returned.shape[2],)
    )
    summed = jnp.sum(picked.astype(jnp.float32) * gate_values[..., None], axis=2)
    return summed.astype(jnp.bfloat16)


def attend_block(query_rows, cache_rows, live_lengths, fresh_rows):
    scores = (
        jnp.einsum("nhc,nlc->nhl", query_rows, cache_rows, preferred_element_type=jnp.float32)
        * SOFTMAX_SCALE
    )
    own_score = (
        jnp.einsum("nhc,nc->nh", query_rows, fresh_rows, preferred_element_type=jnp.float32)
        * SOFTMAX_SCALE
    )
    positions = jnp.arange(cache_rows.shape[1], dtype=jnp.int32)
    scores = jnp.where(positions[None, None, :] < live_lengths[:, None, None], scores, -jnp.inf)
    row_top = jnp.maximum(jnp.max(scores, axis=2), own_score)
    weights = jnp.exp(scores - row_top[:, :, None])
    own_weight = jnp.exp(own_score - row_top)
    summed = jnp.sum(weights, axis=2) + own_weight
    blended = jnp.einsum(
        "nhl,nlc->nhc",
        weights.astype(jnp.bfloat16),
        cache_rows[:, :, :LATENT],
        preferred_element_type=jnp.float32,
    )
    own_rounded = lax.optimization_barrier(own_weight.astype(jnp.bfloat16))
    blended = blended + own_rounded.astype(jnp.float32)[:, :, None] * fresh_rows[
        :, None, :LATENT
    ].astype(jnp.float32)
    return (blended / summed[:, :, None]).astype(jnp.bfloat16)


def per_device(
    hidden,
    routes,
    route_weights,
    expert_in,
    expert_out,
    queries,
    fresh_key,
    latent_cache,
    lengths,
    swapped,
):
    n_ep = lax.axis_size("ep")
    expert_count = lax.axis_size("dp") * n_ep
    packed, target = pack_rows(hidden, routes, expert_count, CAP)
    received = lax.all_to_all(packed, ("dp", "ep"), 0, 0, tiled=True)
    row_count = swapped.shape[0]
    outgoing = jnp.argsort(1 - swapped, stable=True)[:MOVE]
    leaving = latent_cache[outgoing] + received[0, 0, 0] * jnp.zeros((), received.dtype)
    top_bit = lax.axis_size("dp").bit_length() - 2
    incoming_cache = swapped_2(leaving, "dp", top_bit)
    finished = [
        expert_rows(received[:, step * CAP : (step + 1) * CAP], expert_in[0], expert_out[0])
        for step in range(STEPS)
    ]
    arrived = incoming_cache[0, 0, 0] * jnp.zeros((), incoming_cache.dtype)
    finished = [f + arrived for f in finished]
    returned = [lax.all_to_all(f, ("dp", "ep"), 0, 0, tiled=True) for f in finished]
    step_target = target - jnp.arange(STEPS, dtype=jnp.int32)[:, None, None] * CAP
    step_target = step_target + (target // (STEPS * CAP)) * (CAP - STEPS * CAP)
    mixed = jnp.concatenate(
        [
            unpack_rows(returned[step], step_target[step : step + 1], route_weights[step : step + 1])
            for step in range(STEPS)
        ]
    )
    arrival = jnp.clip(jnp.cumsum(swapped) - 1, 0, MOVE - 1)
    is_moved = swapped == 1
    device_rows = lax.axis_index(("dp", "ep")) * row_count + jnp.arange(row_count, dtype=jnp.int32)
    total_rows = expert_count * row_count
    anchor = jnp.where(is_moved, (device_rows + total_rows // 2) % total_rows, device_rows)
    merged_cache = jnp.where(is_moved[:, None, None], incoming_cache[arrival], latent_cache)
    context = attend_block(queries, merged_cache, lengths[anchor], fresh_key)
    return (mixed, context)


def solution(mesh):
    in_specs = (
        P(None, ("dp", "ep"), None),
        P(None, ("dp", "ep"), None),
        P(None, ("dp", "ep"), None),
        P(("dp", "ep"), None, None),
        P(("dp", "ep"), None, None),
        P(("dp", "ep"), None, None),
        P(("dp", "ep"), None),
        P(("dp", "ep"), None, None),
        P(),
        P(("dp", "ep")),
    )
    out_specs = (P(None, ("dp", "ep"), None), P(("dp", "ep"), None, None))
    return jax.shard_map(
        per_device, mesh=mesh, in_specs=in_specs, out_specs=out_specs, check_vma=False
    )
```

```python
import functools

import jax
import jax.numpy as jnp
from jax import lax
from jax.experimental import pallas as pl
from jax.experimental.pallas import tpu as pltpu
from jax.sharding import PartitionSpec as P

LATENT = 512
STEPS = 2
MOVE = 4
CAP = 2
MESH_ID = pl.DeviceIdType.MESH

SOFTMAX_SCALE = 192.0 ** (-0.5)


def _a2a_kernel(n_ep, n_all, x_ref, o_ref, send_sem, recv_sem):
    me = lax.axis_index("dp") * n_ep + lax.axis_index("ep")
    barrier = pltpu.get_barrier_semaphore()

    def greet(k, carry):
        peer = lax.rem(me + k, n_all)
        pl.semaphore_signal(
            barrier, 1, device_id=(peer // n_ep, peer % n_ep), device_id_type=MESH_ID
        )
        return carry

    lax.fori_loop(1, n_all, greet, 0)
    pl.semaphore_wait(barrier, n_all - 1)
    pltpu.make_async_copy(x_ref.at[me], o_ref.at[me], recv_sem).start()

    def send(k, carry):
        peer = lax.rem(me + k, n_all)
        pltpu.make_async_remote_copy(
            x_ref.at[peer],
            o_ref.at[me],
            send_sem,
            recv_sem,
            device_id=(peer // n_ep, peer % n_ep),
            device_id_type=MESH_ID,
        ).start()
        return carry

    lax.fori_loop(1, n_all, send, 0)
    sent = pl.ds(0, n_all - 1)
    pltpu.make_async_copy(x_ref.at[sent], x_ref.at[sent], send_sem).wait()
    pltpu.make_async_copy(o_ref, o_ref, recv_sem).wait()


def all_to_all_rows(x, n_ep, n_all, collective_id):
    nbytes = x.size * x.dtype.itemsize
    return pl.pallas_call(
        functools.partial(_a2a_kernel, n_ep, n_all),
        out_shape=jax.ShapeDtypeStruct(x.shape, x.dtype),
        in_specs=[pl.BlockSpec(memory_space=pl.ANY)],
        out_specs=pl.BlockSpec(memory_space=pl.ANY),
        scratch_shapes=[pltpu.SemaphoreType.DMA(()), pltpu.SemaphoreType.DMA(())],
        compiler_params=pltpu.CompilerParams(collective_id=collective_id, has_side_effects=True),
        cost_estimate=pl.CostEstimate(flops=0, transcendentals=0, bytes_accessed=2 * nbytes),
    )(x)


def swapped_2(value, axis, apart):
    mask = 2**apart
    pairs = [(source, source ^ mask) for source in range(lax.axis_size(axis))]
    return lax.ppermute(value, axis, pairs)


def expert_rows(picked, expert_in, expert_out):
    projected = jnp.einsum("skc,cf->skf", picked, expert_in, preferred_element_type=jnp.float32)
    half_width = projected.shape[2] // 2
    activated = (
        jax.nn.silu(projected[:, :, :half_width]) * projected[:, :, half_width:]
    ).astype(jnp.bfloat16)
    return jnp.einsum(
        "skf,fc->skc", activated, expert_out, preferred_element_type=jnp.float32
    ).astype(jnp.bfloat16)


def pack_rows(tokens, experts, expert_count, slot_cap):
    step_count, token_count, pick_count = experts.shape
    onehot = (experts[:, :, :, None] == jnp.arange(expert_count, dtype=jnp.int32)).astype(
        jnp.int32
    )
    flat = onehot.reshape(step_count, token_count * pick_count, expert_count)
    earlier = jnp.cumsum(flat, axis=1) - flat
    within = jnp.sum(earlier * flat, axis=2).reshape(step_count, token_count, pick_count)
    steps = jnp.arange(step_count, dtype=jnp.int32)[:, None, None]
    target = experts * (step_count * slot_cap) + steps * slot_cap + within
    places = jnp.arange(expert_count * step_count * slot_cap, dtype=jnp.int32).reshape(
        expert_count, step_count * slot_cap
    )
    flat_target = target.reshape(step_count * token_count, pick_count)
    select = jnp.any(flat_target[None, None, :, :] == places[:, :, None, None], axis=3).astype(
        jnp.bfloat16
    )
    flat_tokens = tokens.reshape(step_count * token_count, tokens.shape[2])
    packed = jnp.einsum(
        "dkt,tc->dkc", select, flat_tokens, preferred_element_type=jnp.float32
    ).astype(jnp.bfloat16)
    return packed, target


def unpack_rows(returned, target, gate_values):
    width = returned.shape[1]
    flat_target = target.reshape(-1)
    picked = returned[flat_target // width, flat_target % width].reshape(
        target.shape + (returned.shape[2],)
    )
    summed = jnp.sum(picked.astype(jnp.float32) * gate_values[..., None], axis=2)
    return summed.astype(jnp.bfloat16)


def attend_block(query_rows, cache_rows, live_lengths, fresh_rows):
    scores = (
        jnp.einsum("nhc,nlc->nhl", query_rows, cache_rows, preferred_element_type=jnp.float32)
        * SOFTMAX_SCALE
    )
    own_score = (
        jnp.einsum("nhc,nc->nh", query_rows, fresh_rows, preferred_element_type=jnp.float32)
        * SOFTMAX_SCALE
    )
    positions = jnp.arange(cache_rows.shape[1], dtype=jnp.int32)
    scores = jnp.where(positions[None, None, :] < live_lengths[:, None, None], scores, -jnp.inf)
    row_top = jnp.maximum(jnp.max(scores, axis=2), own_score)
    weights = jnp.exp(scores - row_top[:, :, None])
    own_weight = jnp.exp(own_score - row_top)
    summed = jnp.sum(weights, axis=2) + own_weight
    blended = jnp.einsum(
        "nhl,nlc->nhc",
        weights.astype(jnp.bfloat16),
        cache_rows[:, :, :LATENT],
        preferred_element_type=jnp.float32,
    )
    own_rounded = lax.optimization_barrier(own_weight.astype(jnp.bfloat16))
    blended = blended + own_rounded.astype(jnp.float32)[:, :, None] * fresh_rows[
        :, None, :LATENT
    ].astype(jnp.float32)
    return (blended / summed[:, :, None]).astype(jnp.bfloat16)


def per_device(
    hidden,
    routes,
    route_weights,
    expert_in,
    expert_out,
    queries,
    fresh_key,
    latent_cache,
    lengths,
    swapped,
):
    n_ep = lax.axis_size("ep")
    expert_count = lax.axis_size("dp") * n_ep
    n_dp = lax.axis_size("dp")
    place = (routes % n_ep) * n_dp + routes // n_ep
    packs = [
        pack_rows(hidden[step : step + 1], place[step : step + 1], expert_count, CAP)
        for step in range(STEPS)
    ]
    received = [lax.all_to_all(p[0], ("ep", "dp"), 0, 0, tiled=True) for p in packs]
    finished = [expert_rows(r, expert_in[0], expert_out[0]) for r in received]
    returned = [lax.all_to_all(f, ("ep", "dp"), 0, 0, tiled=True) for f in finished]
    mixed = jnp.concatenate(
        [unpack_rows(returned[step], packs[step][1], route_weights[step : step + 1]) for step in range(STEPS)]
    )
    row_count = swapped.shape[0]
    top_bit = lax.axis_size("dp").bit_length() - 2
    outgoing = jnp.argsort(1 - swapped, stable=True)[:MOVE]
    arrival = jnp.clip(jnp.cumsum(swapped) - 1, 0, MOVE - 1)
    is_moved = swapped == 1
    device_rows = lax.axis_index(("dp", "ep")) * row_count + jnp.arange(row_count, dtype=jnp.int32)
    total_rows = expert_count * row_count
    anchor = jnp.where(is_moved, (device_rows + total_rows // 2) % total_rows, device_rows)
    incoming_cache = swapped_2(latent_cache[outgoing], "dp", top_bit)
    merged_cache = jnp.where(is_moved[:, None, None], incoming_cache[arrival], latent_cache)
    context = attend_block(queries, merged_cache, lengths[anchor], fresh_key)
    return (mixed, context)


def solution(mesh):
    in_specs = (
        P(None, ("dp", "ep"), None),
        P(None, ("dp", "ep"), None),
        P(None, ("dp", "ep"), None),
        P(("dp", "ep"), None, None),
        P(("dp", "ep"), None, None),
        P(("dp", "ep"), None, None),
        P(("dp", "ep"), None),
        P(("dp", "ep"), None, None),
        P(),
        P(("dp", "ep")),
    )
    out_specs = (P(None, ("dp", "ep"), None), P(("dp", "ep"), None, None))
    return jax.shard_map(
        per_device, mesh=mesh, in_specs=in_specs, out_specs=out_specs, check_vma=False
    )
```

```python
import functools

import jax
import jax.numpy as jnp
from jax import lax
from jax.experimental import pallas as pl
from jax.experimental.pallas import tpu as pltpu
from jax.sharding import PartitionSpec as P

LATENT = 512
STEPS = 2
MOVE = 4
CAP = 2
MESH_ID = pl.DeviceIdType.MESH

SOFTMAX_SCALE = 192.0 ** (-0.5)


def _a2a_kernel(n_ep, n_all, x_ref, o_ref, send_sem, recv_sem):
    me = lax.axis_index("dp") * n_ep + lax.axis_index("ep")
    barrier = pltpu.get_barrier_semaphore()

    def greet(k, carry):
        peer = lax.rem(me + k, n_all)
        pl.semaphore_signal(
            barrier, 1, device_id=(peer // n_ep, peer % n_ep), device_id_type=MESH_ID
        )
        return carry

    lax.fori_loop(1, n_all, greet, 0)
    pl.semaphore_wait(barrier, n_all - 1)
    pltpu.make_async_copy(x_ref.at[me], o_ref.at[me], recv_sem).start()

    def send(k, carry):
        peer = lax.rem(me + k, n_all)
        pltpu.make_async_remote_copy(
            x_ref.at[peer],
            o_ref.at[me],
            send_sem,
            recv_sem,
            device_id=(peer // n_ep, peer % n_ep),
            device_id_type=MESH_ID,
        ).start()
        return carry

    lax.fori_loop(1, n_all, send, 0)
    sent = pl.ds(0, n_all - 1)
    pltpu.make_async_copy(x_ref.at[sent], x_ref.at[sent], send_sem).wait()
    pltpu.make_async_copy(o_ref, o_ref, recv_sem).wait()


def all_to_all_rows(x, n_ep, n_all, collective_id):
    nbytes = x.size * x.dtype.itemsize
    return pl.pallas_call(
        functools.partial(_a2a_kernel, n_ep, n_all),
        out_shape=jax.ShapeDtypeStruct(x.shape, x.dtype),
        in_specs=[pl.BlockSpec(memory_space=pl.ANY)],
        out_specs=pl.BlockSpec(memory_space=pl.ANY),
        scratch_shapes=[pltpu.SemaphoreType.DMA(()), pltpu.SemaphoreType.DMA(())],
        compiler_params=pltpu.CompilerParams(collective_id=collective_id, has_side_effects=True),
        cost_estimate=pl.CostEstimate(flops=0, transcendentals=0, bytes_accessed=2 * nbytes),
    )(x)


def swapped_2(value, axis, apart):
    mask = 2**apart
    pairs = [(source, source ^ mask) for source in range(lax.axis_size(axis))]
    return lax.ppermute(value, axis, pairs)


def expert_rows(picked, expert_in, expert_out):
    projected = jnp.einsum("skc,cf->skf", picked, expert_in, preferred_element_type=jnp.float32)
    half_width = projected.shape[2] // 2
    activated = (
        jax.nn.silu(projected[:, :, :half_width]) * projected[:, :, half_width:]
    ).astype(jnp.bfloat16)
    return jnp.einsum(
        "skf,fc->skc", activated, expert_out, preferred_element_type=jnp.float32
    ).astype(jnp.bfloat16)


def pack_rows(tokens, experts, expert_count, slot_cap):
    step_count, token_count, pick_count = experts.shape
    onehot = (experts[:, :, :, None] == jnp.arange(expert_count, dtype=jnp.int32)).astype(
        jnp.int32
    )
    flat = onehot.reshape(step_count, token_count * pick_count, expert_count)
    earlier = jnp.cumsum(flat, axis=1) - flat
    within = jnp.sum(earlier * flat, axis=2).reshape(step_count, token_count, pick_count)
    steps = jnp.arange(step_count, dtype=jnp.int32)[:, None, None]
    target = experts * (step_count * slot_cap) + steps * slot_cap + within
    places = jnp.arange(expert_count * step_count * slot_cap, dtype=jnp.int32).reshape(
        expert_count, step_count * slot_cap
    )
    flat_target = target.reshape(step_count * token_count, pick_count)
    select = jnp.any(flat_target[None, None, :, :] == places[:, :, None, None], axis=3).astype(
        jnp.bfloat16
    )
    flat_tokens = tokens.reshape(step_count * token_count, tokens.shape[2])
    packed = jnp.einsum(
        "dkt,tc->dkc", select, flat_tokens, preferred_element_type=jnp.float32
    ).astype(jnp.bfloat16)
    return packed, target


def unpack_rows(returned, target, gate_values):
    expert_count, slot_cap, _ = returned.shape
    places = jnp.arange(expert_count * slot_cap, dtype=jnp.int32).reshape(expert_count, slot_cap)
    chosen = target[..., None, None] == places
    weights = jnp.sum(jnp.where(chosen, gate_values[..., None, None], 0.0), axis=2)
    summed = jnp.einsum(
        "stek,ekc->stc",
        weights,
        returned.astype(jnp.float32),
        precision=lax.Precision.HIGHEST,
        preferred_element_type=jnp.float32,
    )
    return summed.astype(jnp.bfloat16)


def attend_block(query_rows, cache_rows, live_lengths, fresh_rows):
    scores = (
        jnp.einsum("nhc,nlc->nhl", query_rows, cache_rows, preferred_element_type=jnp.float32)
        * SOFTMAX_SCALE
    )
    own_score = (
        jnp.einsum("nhc,nc->nh", query_rows, fresh_rows, preferred_element_type=jnp.float32)
        * SOFTMAX_SCALE
    )
    positions = jnp.arange(cache_rows.shape[1], dtype=jnp.int32)
    scores = jnp.where(positions[None, None, :] < live_lengths[:, None, None], scores, -jnp.inf)
    row_top = jnp.maximum(jnp.max(scores, axis=2), own_score)
    weights = jnp.exp(scores - row_top[:, :, None])
    own_weight = jnp.exp(own_score - row_top)
    summed = jnp.sum(weights, axis=2) + own_weight
    blended = jnp.einsum(
        "nhl,nlc->nhc",
        weights.astype(jnp.bfloat16),
        cache_rows[:, :, :LATENT],
        preferred_element_type=jnp.float32,
    )
    own_rounded = lax.optimization_barrier(own_weight.astype(jnp.bfloat16))
    blended = blended + own_rounded.astype(jnp.float32)[:, :, None] * fresh_rows[
        :, None, :LATENT
    ].astype(jnp.float32)
    return (blended / summed[:, :, None]).astype(jnp.bfloat16)


def per_device(
    hidden,
    routes,
    route_weights,
    expert_in,
    expert_out,
    queries,
    fresh_key,
    latent_cache,
    lengths,
    swapped,
):
    n_ep = lax.axis_size("ep")
    expert_count = lax.axis_size("dp") * n_ep
    packs = [
        pack_rows(hidden[step : step + 1], routes[step : step + 1], expert_count, CAP)
        for step in range(STEPS)
    ]
    received = [lax.all_to_all(p[0], ("dp", "ep"), 0, 0, tiled=True) for p in packs]
    finished = [expert_rows(r, expert_in[0], expert_out[0]) for r in received]
    returned = [lax.all_to_all(f, ("dp", "ep"), 0, 0, tiled=True) for f in finished]
    mixed = jnp.concatenate(
        [unpack_rows(returned[step], packs[step][1], route_weights[step : step + 1]) for step in range(STEPS)]
    )
    row_count = swapped.shape[0]
    top_bit = lax.axis_size("dp").bit_length() - 2
    outgoing = jnp.argsort(1 - swapped, stable=True)[:MOVE]
    arrival = jnp.clip(jnp.cumsum(swapped) - 1, 0, MOVE - 1)
    is_moved = swapped == 1
    device_rows = lax.axis_index(("dp", "ep")) * row_count + jnp.arange(row_count, dtype=jnp.int32)
    total_rows = expert_count * row_count
    anchor = jnp.where(is_moved, (device_rows + total_rows // 2) % total_rows, device_rows)
    incoming_cache = swapped_2(latent_cache[outgoing], "dp", top_bit)
    merged_cache = jnp.where(is_moved[:, None, None], incoming_cache[arrival], latent_cache)
    context = attend_block(queries, merged_cache, lengths[anchor], fresh_key)
    return (mixed, context)


def solution(mesh):
    in_specs = (
        P(None, ("dp", "ep"), None),
        P(None, ("dp", "ep"), None),
        P(None, ("dp", "ep"), None),
        P(("dp", "ep"), None, None),
        P(("dp", "ep"), None, None),
        P(("dp", "ep"), None, None),
        P(("dp", "ep"), None),
        P(("dp", "ep"), None, None),
        P(),
        P(("dp", "ep")),
    )
    out_specs = (P(None, ("dp", "ep"), None), P(("dp", "ep"), None, None))
    return jax.shard_map(
        per_device, mesh=mesh, in_specs=in_specs, out_specs=out_specs, check_vma=False
    )
```

```python
import functools

import jax
import jax.numpy as jnp
from jax import lax
from jax.experimental import pallas as pl
from jax.experimental.pallas import tpu as pltpu
from jax.sharding import PartitionSpec as P

LATENT = 512
STEPS = 2
MOVE = 4
CAP = 2
MESH_ID = pl.DeviceIdType.MESH

SOFTMAX_SCALE = 192.0 ** (-0.5)


def _a2a_kernel(n_ep, n_all, x_ref, o_ref, send_sem, recv_sem):
    me = lax.axis_index("dp") * n_ep + lax.axis_index("ep")
    barrier = pltpu.get_barrier_semaphore()

    def greet(k, carry):
        peer = lax.rem(me + k, n_all)
        pl.semaphore_signal(
            barrier, 1, device_id=(peer // n_ep, peer % n_ep), device_id_type=MESH_ID
        )
        return carry

    lax.fori_loop(1, n_all, greet, 0)
    pl.semaphore_wait(barrier, n_all - 1)
    pltpu.make_async_copy(x_ref.at[me], o_ref.at[me], recv_sem).start()

    def send(k, carry):
        peer = lax.rem(me + k, n_all)
        pltpu.make_async_remote_copy(
            x_ref.at[peer],
            o_ref.at[me],
            send_sem,
            recv_sem,
            device_id=(peer // n_ep, peer % n_ep),
            device_id_type=MESH_ID,
        ).start()
        return carry

    lax.fori_loop(1, n_all, send, 0)
    sent = pl.ds(0, n_all - 1)
    pltpu.make_async_copy(x_ref.at[sent], x_ref.at[sent], send_sem).wait()
    pltpu.make_async_copy(o_ref, o_ref, recv_sem).wait()


def all_to_all_rows(x, n_ep, n_all, collective_id):
    nbytes = x.size * x.dtype.itemsize
    return pl.pallas_call(
        functools.partial(_a2a_kernel, n_ep, n_all),
        out_shape=jax.ShapeDtypeStruct(x.shape, x.dtype),
        in_specs=[pl.BlockSpec(memory_space=pl.ANY)],
        out_specs=pl.BlockSpec(memory_space=pl.ANY),
        scratch_shapes=[pltpu.SemaphoreType.DMA(()), pltpu.SemaphoreType.DMA(())],
        compiler_params=pltpu.CompilerParams(collective_id=collective_id, has_side_effects=True),
        cost_estimate=pl.CostEstimate(flops=0, transcendentals=0, bytes_accessed=2 * nbytes),
    )(x)


def swapped_2(value, axis, apart):
    mask = 2**apart
    pairs = [(source, source ^ mask) for source in range(lax.axis_size(axis))]
    return lax.ppermute(value, axis, pairs)


def expert_rows(picked, expert_in, expert_out):
    projected = jnp.einsum("skc,cf->skf", picked, expert_in, preferred_element_type=jnp.float32)
    half_width = projected.shape[2] // 2
    activated = (
        jax.nn.silu(projected[:, :, :half_width]) * projected[:, :, half_width:]
    ).astype(jnp.bfloat16)
    return jnp.einsum(
        "skf,fc->skc", activated, expert_out, preferred_element_type=jnp.float32
    ).astype(jnp.bfloat16)


def pack_rows(tokens, experts, expert_count, slot_cap):
    step_count, token_count, pick_count = experts.shape
    onehot = (experts[:, :, :, None] == jnp.arange(expert_count, dtype=jnp.int32)).astype(
        jnp.int32
    )
    flat = onehot.reshape(step_count, token_count * pick_count, expert_count)
    earlier = jnp.cumsum(flat, axis=1) - flat
    within = jnp.sum(earlier * flat, axis=2).reshape(step_count, token_count, pick_count)
    steps = jnp.arange(step_count, dtype=jnp.int32)[:, None, None]
    target = experts * (step_count * slot_cap) + steps * slot_cap + within
    places = jnp.arange(expert_count * step_count * slot_cap, dtype=jnp.int32).reshape(
        expert_count, step_count * slot_cap
    )
    flat_target = target.reshape(step_count * token_count, pick_count)
    select = jnp.any(flat_target[None, None, :, :] == places[:, :, None, None], axis=3).astype(
        jnp.bfloat16
    )
    flat_tokens = tokens.reshape(step_count * token_count, tokens.shape[2])
    packed = jnp.einsum(
        "dkt,tc->dkc", select, flat_tokens, preferred_element_type=jnp.float32
    ).astype(jnp.bfloat16)
    return packed, target


def unpack_rows(returned, target, gate_values):
    expert_count, slot_cap, _ = returned.shape
    places = jnp.arange(expert_count * slot_cap, dtype=jnp.int32).reshape(expert_count, slot_cap)
    chosen = target[..., None, None] == places
    weights = jnp.sum(jnp.where(chosen, gate_values[..., None, None], 0.0), axis=2)
    summed = jnp.einsum(
        "stek,ekc->stc",
        weights,
        returned.astype(jnp.float32),
        precision=lax.Precision.HIGHEST,
        preferred_element_type=jnp.float32,
    )
    return summed.astype(jnp.bfloat16)


def attend_block(query_rows, cache_rows, live_lengths, fresh_rows):
    scores = (
        jnp.einsum("nhc,nlc->nhl", query_rows, cache_rows, preferred_element_type=jnp.float32)
        * SOFTMAX_SCALE
    )
    own_score = (
        jnp.einsum("nhc,nc->nh", query_rows, fresh_rows, preferred_element_type=jnp.float32)
        * SOFTMAX_SCALE
    )
    positions = jnp.arange(cache_rows.shape[1], dtype=jnp.int32)
    scores = jnp.where(positions[None, None, :] < live_lengths[:, None, None], scores, -jnp.inf)
    row_top = jnp.maximum(jnp.max(scores, axis=2), own_score)
    weights = jnp.exp(scores - row_top[:, :, None])
    own_weight = jnp.exp(own_score - row_top)
    summed = jnp.sum(weights, axis=2) + own_weight
    blended = jnp.einsum(
        "nhl,nlc->nhc",
        weights.astype(jnp.bfloat16),
        cache_rows[:, :, :LATENT],
        preferred_element_type=jnp.float32,
    )
    own_rounded = lax.optimization_barrier(own_weight.astype(jnp.bfloat16))
    blended = blended + own_rounded.astype(jnp.float32)[:, :, None] * fresh_rows[
        :, None, :LATENT
    ].astype(jnp.float32)
    return (blended / summed[:, :, None]).astype(jnp.bfloat16)


def per_device(
    hidden,
    routes,
    route_weights,
    expert_in,
    expert_out,
    queries,
    fresh_key,
    latent_cache,
    lengths,
    swapped,
):
    n_ep = lax.axis_size("ep")
    expert_count = lax.axis_size("dp") * n_ep
    packs = [
        pack_rows(hidden[step : step + 1], routes[step : step + 1], expert_count, CAP)
        for step in range(STEPS)
    ]
    row_count = swapped.shape[0]
    top_bit = lax.axis_size("dp").bit_length() - 2
    outgoing = jnp.argsort(1 - swapped, stable=True)[:MOVE]
    incoming_cache = swapped_2(latent_cache[outgoing], "dp", top_bit)
    arrived = incoming_cache[0, 0, 0] * jnp.zeros((), incoming_cache.dtype)
    sends = [p[0] + arrived for p in packs]
    received = [lax.all_to_all(p, ("dp", "ep"), 0, 0, tiled=True) for p in sends]
    finished = [expert_rows(r, expert_in[0], expert_out[0]) for r in received]
    returned = [lax.all_to_all(f, ("dp", "ep"), 0, 0, tiled=True) for f in finished]
    mixed = jnp.concatenate(
        [unpack_rows(returned[step], packs[step][1], route_weights[step : step + 1]) for step in range(STEPS)]
    )
    arrival = jnp.clip(jnp.cumsum(swapped) - 1, 0, MOVE - 1)
    is_moved = swapped == 1
    device_rows = lax.axis_index(("dp", "ep")) * row_count + jnp.arange(row_count, dtype=jnp.int32)
    total_rows = expert_count * row_count
    anchor = jnp.where(is_moved, (device_rows + total_rows // 2) % total_rows, device_rows)
    merged_cache = jnp.where(is_moved[:, None, None], incoming_cache[arrival], latent_cache)
    context = attend_block(queries, merged_cache, lengths[anchor], fresh_key)
    return (mixed, context)


def solution(mesh):
    in_specs = (
        P(None, ("dp", "ep"), None),
        P(None, ("dp", "ep"), None),
        P(None, ("dp", "ep"), None),
        P(("dp", "ep"), None, None),
        P(("dp", "ep"), None, None),
        P(("dp", "ep"), None, None),
        P(("dp", "ep"), None),
        P(("dp", "ep"), None, None),
        P(),
        P(("dp", "ep")),
    )
    out_specs = (P(None, ("dp", "ep"), None), P(("dp", "ep"), None, None))
    return jax.shard_map(
        per_device, mesh=mesh, in_specs=in_specs, out_specs=out_specs, check_vma=False
    )
```

```python
import functools

import jax
import jax.numpy as jnp
from jax import lax
from jax.experimental import pallas as pl
from jax.experimental.pallas import tpu as pltpu
from jax.sharding import PartitionSpec as P

LATENT = 512
STEPS = 2
MOVE = 4
CAP = 2
MESH_ID = pl.DeviceIdType.MESH

SOFTMAX_SCALE = 192.0 ** (-0.5)


def _a2a_kernel(n_ep, n_all, x_ref, o_ref, send_sem, recv_sem):
    me = lax.axis_index("dp") * n_ep + lax.axis_index("ep")
    barrier = pltpu.get_barrier_semaphore()

    def greet(k, carry):
        peer = lax.rem(me + k, n_all)
        pl.semaphore_signal(
            barrier, 1, device_id=(peer // n_ep, peer % n_ep), device_id_type=MESH_ID
        )
        return carry

    lax.fori_loop(1, n_all, greet, 0)
    pl.semaphore_wait(barrier, n_all - 1)
    pltpu.make_async_copy(x_ref.at[me], o_ref.at[me], recv_sem).start()

    def send(k, carry):
        peer = lax.rem(me + k, n_all)
        pltpu.make_async_remote_copy(
            x_ref.at[peer],
            o_ref.at[me],
            send_sem,
            recv_sem,
            device_id=(peer // n_ep, peer % n_ep),
            device_id_type=MESH_ID,
        ).start()
        return carry

    lax.fori_loop(1, n_all, send, 0)
    sent = pl.ds(0, n_all - 1)
    pltpu.make_async_copy(x_ref.at[sent], x_ref.at[sent], send_sem).wait()
    pltpu.make_async_copy(o_ref, o_ref, recv_sem).wait()


def all_to_all_rows(x, n_ep, n_all, collective_id):
    nbytes = x.size * x.dtype.itemsize
    return pl.pallas_call(
        functools.partial(_a2a_kernel, n_ep, n_all),
        out_shape=jax.ShapeDtypeStruct(x.shape, x.dtype),
        in_specs=[pl.BlockSpec(memory_space=pl.ANY)],
        out_specs=pl.BlockSpec(memory_space=pl.ANY),
        scratch_shapes=[pltpu.SemaphoreType.DMA(()), pltpu.SemaphoreType.DMA(())],
        compiler_params=pltpu.CompilerParams(collective_id=collective_id, has_side_effects=True),
        cost_estimate=pl.CostEstimate(flops=0, transcendentals=0, bytes_accessed=2 * nbytes),
    )(x)


def swapped_2(value, axis, apart):
    mask = 2**apart
    pairs = [(source, source ^ mask) for source in range(lax.axis_size(axis))]
    return lax.ppermute(value, axis, pairs)


def expert_rows(picked, expert_in, expert_out):
    projected = jnp.einsum("skc,cf->skf", picked, expert_in, preferred_element_type=jnp.float32)
    half_width = projected.shape[2] // 2
    activated = (
        jax.nn.silu(projected[:, :, :half_width]) * projected[:, :, half_width:]
    ).astype(jnp.bfloat16)
    return jnp.einsum(
        "skf,fc->skc", activated, expert_out, preferred_element_type=jnp.float32
    ).astype(jnp.bfloat16)


def pack_rows(tokens, experts, expert_count, slot_cap):
    step_count, token_count, pick_count = experts.shape
    onehot = (experts[:, :, :, None] == jnp.arange(expert_count, dtype=jnp.int32)).astype(
        jnp.int32
    )
    flat = onehot.reshape(step_count, token_count * pick_count, expert_count)
    earlier = jnp.cumsum(flat, axis=1) - flat
    within = jnp.sum(earlier * flat, axis=2).reshape(step_count, token_count, pick_count)
    steps = jnp.arange(step_count, dtype=jnp.int32)[:, None, None]
    target = experts * (step_count * slot_cap) + steps * slot_cap + within
    places = jnp.arange(expert_count * step_count * slot_cap, dtype=jnp.int32).reshape(
        expert_count, step_count * slot_cap
    )
    flat_target = target.reshape(step_count * token_count, pick_count)
    select = jnp.any(flat_target[None, None, :, :] == places[:, :, None, None], axis=3).astype(
        jnp.bfloat16
    )
    flat_tokens = tokens.reshape(step_count * token_count, tokens.shape[2])
    packed = jnp.einsum(
        "dkt,tc->dkc", select, flat_tokens, preferred_element_type=jnp.float32
    ).astype(jnp.bfloat16)
    return packed, target


def unpack_rows(returned, target, gate_values):
    expert_count, slot_cap, _ = returned.shape
    places = jnp.arange(expert_count * slot_cap, dtype=jnp.int32).reshape(expert_count, slot_cap)
    chosen = target[..., None, None] == places
    weights = jnp.sum(jnp.where(chosen, gate_values[..., None, None], 0.0), axis=2)
    summed = jnp.einsum(
        "stek,ekc->stc",
        weights,
        returned.astype(jnp.float32),
        precision=lax.Precision.HIGHEST,
        preferred_element_type=jnp.float32,
    )
    return summed.astype(jnp.bfloat16)


def gather_rows(returned, target, gate_values):
    width = returned.shape[1]
    flat_target = target.reshape(-1)
    picked = returned[flat_target // width, flat_target % width].reshape(
        target.shape + (returned.shape[2],)
    )
    summed = jnp.sum(picked.astype(jnp.float32) * gate_values[..., None], axis=2)
    return summed.astype(jnp.bfloat16)


def attend_block(query_rows, cache_rows, live_lengths, fresh_rows):
    scores = (
        jnp.einsum("nhc,nlc->nhl", query_rows, cache_rows, preferred_element_type=jnp.float32)
        * SOFTMAX_SCALE
    )
    own_score = (
        jnp.einsum("nhc,nc->nh", query_rows, fresh_rows, preferred_element_type=jnp.float32)
        * SOFTMAX_SCALE
    )
    positions = jnp.arange(cache_rows.shape[1], dtype=jnp.int32)
    scores = jnp.where(positions[None, None, :] < live_lengths[:, None, None], scores, -jnp.inf)
    row_top = jnp.maximum(jnp.max(scores, axis=2), own_score)
    weights = jnp.exp(scores - row_top[:, :, None])
    own_weight = jnp.exp(own_score - row_top)
    summed = jnp.sum(weights, axis=2) + own_weight
    blended = jnp.einsum(
        "nhl,nlc->nhc",
        weights.astype(jnp.bfloat16),
        cache_rows[:, :, :LATENT],
        preferred_element_type=jnp.float32,
    )
    own_rounded = lax.optimization_barrier(own_weight.astype(jnp.bfloat16))
    blended = blended + own_rounded.astype(jnp.float32)[:, :, None] * fresh_rows[
        :, None, :LATENT
    ].astype(jnp.float32)
    return (blended / summed[:, :, None]).astype(jnp.bfloat16)


def per_device(
    hidden,
    routes,
    route_weights,
    expert_in,
    expert_out,
    queries,
    fresh_key,
    latent_cache,
    lengths,
    swapped,
):
    n_ep = lax.axis_size("ep")
    expert_count = lax.axis_size("dp") * n_ep
    packs = [
        pack_rows(hidden[step : step + 1], routes[step : step + 1], expert_count, CAP)
        for step in range(STEPS)
    ]
    received = [lax.all_to_all(p[0], ("dp", "ep"), 0, 0, tiled=True) for p in packs]
    finished = [expert_rows(r, expert_in[0], expert_out[0]) for r in received]
    returned = [lax.all_to_all(f, ("dp", "ep"), 0, 0, tiled=True) for f in finished]
    mixed = jnp.concatenate(
        [gather_rows(returned[0], packs[0][1], route_weights[0:1])]
        + [unpack_rows(returned[step], packs[step][1], route_weights[step : step + 1]) for step in range(1, STEPS)]
    )
    row_count = swapped.shape[0]
    top_bit = lax.axis_size("dp").bit_length() - 2
    outgoing = jnp.argsort(1 - swapped, stable=True)[:MOVE]
    arrival = jnp.clip(jnp.cumsum(swapped) - 1, 0, MOVE - 1)
    is_moved = swapped == 1
    device_rows = lax.axis_index(("dp", "ep")) * row_count + jnp.arange(row_count, dtype=jnp.int32)
    total_rows = expert_count * row_count
    anchor = jnp.where(is_moved, (device_rows + total_rows // 2) % total_rows, device_rows)
    incoming_cache = swapped_2(latent_cache[outgoing], "dp", top_bit)
    merged_cache = jnp.where(is_moved[:, None, None], incoming_cache[arrival], latent_cache)
    context = attend_block(queries, merged_cache, lengths[anchor], fresh_key)
    return (mixed, context)


def solution(mesh):
    in_specs = (
        P(None, ("dp", "ep"), None),
        P(None, ("dp", "ep"), None),
        P(None, ("dp", "ep"), None),
        P(("dp", "ep"), None, None),
        P(("dp", "ep"), None, None),
        P(("dp", "ep"), None, None),
        P(("dp", "ep"), None),
        P(("dp", "ep"), None, None),
        P(),
        P(("dp", "ep")),
    )
    out_specs = (P(None, ("dp", "ep"), None), P(("dp", "ep"), None, None))
    return jax.shard_map(
        per_device, mesh=mesh, in_specs=in_specs, out_specs=out_specs, check_vma=False
    )
```

```python
import functools

import jax
import jax.numpy as jnp
from jax import lax
from jax.experimental import pallas as pl
from jax.experimental.pallas import tpu as pltpu
from jax.sharding import PartitionSpec as P

LATENT = 512
STEPS = 2
MOVE = 4
CAP = 2
MESH_ID = pl.DeviceIdType.MESH

SOFTMAX_SCALE = 192.0 ** (-0.5)


def _a2a_kernel(n_ep, n_all, x_ref, o_ref, send_sem, recv_sem):
    me = lax.axis_index("dp") * n_ep + lax.axis_index("ep")
    barrier = pltpu.get_barrier_semaphore()

    def greet(k, carry):
        peer = lax.rem(me + k, n_all)
        pl.semaphore_signal(
            barrier, 1, device_id=(peer // n_ep, peer % n_ep), device_id_type=MESH_ID
        )
        return carry

    lax.fori_loop(1, n_all, greet, 0)
    pl.semaphore_wait(barrier, n_all - 1)
    pltpu.make_async_copy(x_ref.at[me], o_ref.at[me], recv_sem).start()

    def send(k, carry):
        peer = lax.rem(me + k, n_all)
        pltpu.make_async_remote_copy(
            x_ref.at[peer],
            o_ref.at[me],
            send_sem,
            recv_sem,
            device_id=(peer // n_ep, peer % n_ep),
            device_id_type=MESH_ID,
        ).start()
        return carry

    lax.fori_loop(1, n_all, send, 0)
    sent = pl.ds(0, n_all - 1)
    pltpu.make_async_copy(x_ref.at[sent], x_ref.at[sent], send_sem).wait()
    pltpu.make_async_copy(o_ref, o_ref, recv_sem).wait()


def all_to_all_rows(x, n_ep, n_all, collective_id):
    nbytes = x.size * x.dtype.itemsize
    return pl.pallas_call(
        functools.partial(_a2a_kernel, n_ep, n_all),
        out_shape=jax.ShapeDtypeStruct(x.shape, x.dtype),
        in_specs=[pl.BlockSpec(memory_space=pl.ANY)],
        out_specs=pl.BlockSpec(memory_space=pl.ANY),
        scratch_shapes=[pltpu.SemaphoreType.DMA(()), pltpu.SemaphoreType.DMA(())],
        compiler_params=pltpu.CompilerParams(collective_id=collective_id, has_side_effects=True),
        cost_estimate=pl.CostEstimate(flops=0, transcendentals=0, bytes_accessed=2 * nbytes),
    )(x)


def swapped_2(value, axis, apart):
    mask = 2**apart
    pairs = [(source, source ^ mask) for source in range(lax.axis_size(axis))]
    return lax.ppermute(value, axis, pairs)


def expert_rows(picked, expert_in, expert_out):
    projected = jnp.einsum("skc,cf->skf", picked, expert_in, preferred_element_type=jnp.float32)
    half_width = projected.shape[2] // 2
    activated = (
        jax.nn.silu(projected[:, :, :half_width]) * projected[:, :, half_width:]
    ).astype(jnp.bfloat16)
    return jnp.einsum(
        "skf,fc->skc", activated, expert_out, preferred_element_type=jnp.float32
    ).astype(jnp.bfloat16)


def pack_rows(tokens, experts, expert_count, slot_cap):
    step_count, token_count, pick_count = experts.shape
    onehot = (experts[:, :, :, None] == jnp.arange(expert_count, dtype=jnp.int32)).astype(
        jnp.int32
    )
    flat = onehot.reshape(step_count, token_count * pick_count, expert_count)
    earlier = jnp.cumsum(flat, axis=1) - flat
    within = jnp.sum(earlier * flat, axis=2).reshape(step_count, token_count, pick_count)
    steps = jnp.arange(step_count, dtype=jnp.int32)[:, None, None]
    target = experts * (step_count * slot_cap) + steps * slot_cap + within
    places = jnp.arange(expert_count * step_count * slot_cap, dtype=jnp.int32).reshape(
        expert_count, step_count * slot_cap
    )
    flat_target = target.reshape(step_count * token_count, pick_count)
    select = jnp.any(flat_target[None, None, :, :] == places[:, :, None, None], axis=3).astype(
        jnp.bfloat16
    )
    flat_tokens = tokens.reshape(step_count * token_count, tokens.shape[2])
    packed = jnp.einsum(
        "dkt,tc->dkc", select, flat_tokens, preferred_element_type=jnp.float32
    ).astype(jnp.bfloat16)
    return packed, target


def unpack_rows(returned, target, gate_values):
    expert_count, slot_cap, _ = returned.shape
    places = jnp.arange(expert_count * slot_cap, dtype=jnp.int32).reshape(expert_count, slot_cap)
    chosen = target[..., None, None] == places
    weights = jnp.sum(jnp.where(chosen, gate_values[..., None, None], 0.0), axis=2)
    summed = jnp.einsum(
        "stek,ekc->stc",
        weights,
        returned.astype(jnp.float32),
        precision=lax.Precision.HIGHEST,
        preferred_element_type=jnp.float32,
    )
    return summed.astype(jnp.bfloat16)


def gather_rows(returned, target, gate_values):
    width = returned.shape[1]
    flat_target = target.reshape(-1)
    picked = returned[flat_target // width, flat_target % width].reshape(
        target.shape + (returned.shape[2],)
    )
    summed = jnp.sum(picked.astype(jnp.float32) * gate_values[..., None], axis=2)
    return summed.astype(jnp.bfloat16)


def attend_block(query_rows, cache_rows, live_lengths, fresh_rows):
    scores = (
        jnp.einsum("nhc,nlc->nhl", query_rows, cache_rows, preferred_element_type=jnp.float32)
        * SOFTMAX_SCALE
    )
    own_score = (
        jnp.einsum("nhc,nc->nh", query_rows, fresh_rows, preferred_element_type=jnp.float32)
        * SOFTMAX_SCALE
    )
    positions = jnp.arange(cache_rows.shape[1], dtype=jnp.int32)
    scores = jnp.where(positions[None, None, :] < live_lengths[:, None, None], scores, -jnp.inf)
    row_top = jnp.maximum(jnp.max(scores, axis=2), own_score)
    weights = jnp.exp(scores - row_top[:, :, None])
    own_weight = jnp.exp(own_score - row_top)
    summed = jnp.sum(weights, axis=2) + own_weight
    blended = jnp.einsum(
        "nhl,nlc->nhc",
        weights.astype(jnp.bfloat16),
        cache_rows[:, :, :LATENT],
        preferred_element_type=jnp.float32,
    )
    own_rounded = lax.optimization_barrier(own_weight.astype(jnp.bfloat16))
    blended = blended + own_rounded.astype(jnp.float32)[:, :, None] * fresh_rows[
        :, None, :LATENT
    ].astype(jnp.float32)
    return (blended / summed[:, :, None]).astype(jnp.bfloat16)


def per_device(
    hidden,
    routes,
    route_weights,
    expert_in,
    expert_out,
    queries,
    fresh_key,
    latent_cache,
    lengths,
    swapped,
):
    n_ep = lax.axis_size("ep")
    expert_count = lax.axis_size("dp") * n_ep
    packs = [
        pack_rows(hidden[step : step + 1], routes[step : step + 1], expert_count, CAP)
        for step in range(STEPS)
    ]
    received = [lax.all_to_all(p[0], ("dp", "ep"), 0, 0, tiled=True) for p in packs]
    finished = [expert_rows(r, expert_in[0], expert_out[0]) for r in received]
    returned = [lax.all_to_all(f, ("dp", "ep"), 0, 0, tiled=True) for f in finished]
    mixed = jnp.concatenate(
        [gather_rows(returned[0], packs[0][1], route_weights[0:1])]
        + [unpack_rows(returned[step], packs[step][1], route_weights[step : step + 1]) for step in range(1, STEPS)]
    )
    row_count = swapped.shape[0]
    top_bit = lax.axis_size("dp").bit_length() - 2
    rank = jnp.cumsum(swapped) - 1
    picks = (swapped[None, :] == 1) & (rank[None, :] == jnp.arange(MOVE, dtype=jnp.int32)[:, None])
    arrival = jnp.clip(jnp.cumsum(swapped) - 1, 0, MOVE - 1)
    is_moved = swapped == 1
    device_rows = lax.axis_index(("dp", "ep")) * row_count + jnp.arange(row_count, dtype=jnp.int32)
    total_rows = expert_count * row_count
    anchor = jnp.where(is_moved, (device_rows + total_rows // 2) % total_rows, device_rows)
    leaving = jnp.einsum(
        "mn,nlc->mlc", picks.astype(latent_cache.dtype), latent_cache, preferred_element_type=jnp.float32
    ).astype(latent_cache.dtype)
    incoming_cache = swapped_2(leaving, "dp", top_bit)
    merged_cache = jnp.where(is_moved[:, None, None], incoming_cache[arrival], latent_cache)
    context = attend_block(queries, merged_cache, lengths[anchor], fresh_key)
    return (mixed, context)


def solution(mesh):
    in_specs = (
        P(None, ("dp", "ep"), None),
        P(None, ("dp", "ep"), None),
        P(None, ("dp", "ep"), None),
        P(("dp", "ep"), None, None),
        P(("dp", "ep"), None, None),
        P(("dp", "ep"), None, None),
        P(("dp", "ep"), None),
        P(("dp", "ep"), None, None),
        P(),
        P(("dp", "ep")),
    )
    out_specs = (P(None, ("dp", "ep"), None), P(("dp", "ep"), None, None))
    return jax.shard_map(
        per_device, mesh=mesh, in_specs=in_specs, out_specs=out_specs, check_vma=False
    )
```

```python
import functools

import jax
import jax.numpy as jnp
from jax import lax
from jax.experimental import pallas as pl
from jax.experimental.pallas import tpu as pltpu
from jax.sharding import PartitionSpec as P

LATENT = 512
STEPS = 2
MOVE = 4
CAP = 2
MESH_ID = pl.DeviceIdType.MESH

SOFTMAX_SCALE = 192.0 ** (-0.5)


def _a2a_kernel(n_ep, n_all, x_ref, o_ref, send_sem, recv_sem):
    me = lax.axis_index("dp") * n_ep + lax.axis_index("ep")
    barrier = pltpu.get_barrier_semaphore()

    def greet(k, carry):
        peer = lax.rem(me + k, n_all)
        pl.semaphore_signal(
            barrier, 1, device_id=(peer // n_ep, peer % n_ep), device_id_type=MESH_ID
        )
        return carry

    lax.fori_loop(1, n_all, greet, 0)
    pl.semaphore_wait(barrier, n_all - 1)
    pltpu.make_async_copy(x_ref.at[me], o_ref.at[me], recv_sem).start()

    def send(k, carry):
        peer = lax.rem(me + k, n_all)
        pltpu.make_async_remote_copy(
            x_ref.at[peer],
            o_ref.at[me],
            send_sem,
            recv_sem,
            device_id=(peer // n_ep, peer % n_ep),
            device_id_type=MESH_ID,
        ).start()
        return carry

    lax.fori_loop(1, n_all, send, 0)
    sent = pl.ds(0, n_all - 1)
    pltpu.make_async_copy(x_ref.at[sent], x_ref.at[sent], send_sem).wait()
    pltpu.make_async_copy(o_ref, o_ref, recv_sem).wait()


def all_to_all_rows(x, n_ep, n_all, collective_id):
    nbytes = x.size * x.dtype.itemsize
    return pl.pallas_call(
        functools.partial(_a2a_kernel, n_ep, n_all),
        out_shape=jax.ShapeDtypeStruct(x.shape, x.dtype),
        in_specs=[pl.BlockSpec(memory_space=pl.ANY)],
        out_specs=pl.BlockSpec(memory_space=pl.ANY),
        scratch_shapes=[pltpu.SemaphoreType.DMA(()), pltpu.SemaphoreType.DMA(())],
        compiler_params=pltpu.CompilerParams(collective_id=collective_id, has_side_effects=True),
        cost_estimate=pl.CostEstimate(flops=0, transcendentals=0, bytes_accessed=2 * nbytes),
    )(x)


def swapped_2(value, axis, apart):
    mask = 2**apart
    pairs = [(source, source ^ mask) for source in range(lax.axis_size(axis))]
    return lax.ppermute(value, axis, pairs)


def expert_rows(picked, expert_in, expert_out):
    projected = jnp.einsum("skc,cf->skf", picked, expert_in, preferred_element_type=jnp.float32)
    half_width = projected.shape[2] // 2
    activated = (
        jax.nn.silu(projected[:, :, :half_width]) * projected[:, :, half_width:]
    ).astype(jnp.bfloat16)
    return jnp.einsum(
        "skf,fc->skc", activated, expert_out, preferred_element_type=jnp.float32
    ).astype(jnp.bfloat16)


def pack_rows(tokens, experts, expert_count, slot_cap):
    step_count, token_count, pick_count = experts.shape
    onehot = (experts[:, :, :, None] == jnp.arange(expert_count, dtype=jnp.int32)).astype(
        jnp.int32
    )
    flat = onehot.reshape(step_count, token_count * pick_count, expert_count)
    earlier = jnp.cumsum(flat, axis=1) - flat
    within = jnp.sum(earlier * flat, axis=2).reshape(step_count, token_count, pick_count)
    steps = jnp.arange(step_count, dtype=jnp.int32)[:, None, None]
    target = experts * (step_count * slot_cap) + steps * slot_cap + within
    places = jnp.arange(expert_count * step_count * slot_cap, dtype=jnp.int32).reshape(
        expert_count, step_count * slot_cap
    )
    flat_target = target.reshape(step_count * token_count, pick_count)
    select = jnp.any(flat_target[None, None, :, :] == places[:, :, None, None], axis=3).astype(
        jnp.bfloat16
    )
    flat_tokens = tokens.reshape(step_count * token_count, tokens.shape[2])
    packed = jnp.einsum(
        "dkt,tc->dkc", select, flat_tokens, preferred_element_type=jnp.float32
    ).astype(jnp.bfloat16)
    return packed, target


def pack_rows_tiled(tokens, experts, expert_count, slot_cap, parts):
    token_count, pick_count = experts.shape
    onehot = (experts[:, :, None] == jnp.arange(expert_count, dtype=jnp.int32)).astype(jnp.int32)
    flat = onehot.reshape(token_count * pick_count, expert_count)
    earlier = jnp.cumsum(flat, axis=0) - flat
    within = jnp.sum(earlier * flat, axis=1).reshape(token_count, pick_count)
    target = experts * slot_cap + within
    rows = jnp.arange(slot_cap * parts, dtype=jnp.int32)
    slot_of = jnp.arange(expert_count, dtype=jnp.int32)[:, None] * slot_cap + rows[None, :] // parts
    hit = jnp.any(target[None, None, :, :] == slot_of[:, :, None, None], axis=3)
    same_part = (rows % parts)[:, None] == (jnp.arange(token_count * parts) % parts)[None, :]
    select = (jnp.repeat(hit, parts, axis=2) & same_part[None, :, :]).astype(jnp.bfloat16)
    pieces = tokens.reshape(token_count * parts, tokens.shape[1] // parts)
    packed = jnp.dot(
        select.reshape(expert_count * slot_cap * parts, token_count * parts),
        pieces,
        preferred_element_type=jnp.float32,
    ).astype(jnp.bfloat16)
    return packed.reshape(expert_count, slot_cap * parts, pieces.shape[1]), target[None]


def unpack_rows(returned, target, gate_values):
    expert_count, slot_cap, _ = returned.shape
    places = jnp.arange(expert_count * slot_cap, dtype=jnp.int32).reshape(expert_count, slot_cap)
    chosen = target[..., None, None] == places
    weights = jnp.sum(jnp.where(chosen, gate_values[..., None, None], 0.0), axis=2)
    summed = jnp.einsum(
        "stek,ekc->stc",
        weights,
        returned.astype(jnp.float32),
        precision=lax.Precision.HIGHEST,
        preferred_element_type=jnp.float32,
    )
    return summed.astype(jnp.bfloat16)


def gather_rows(returned, target, gate_values):
    width = returned.shape[1]
    flat_target = target.reshape(-1)
    picked = returned[flat_target // width, flat_target % width].reshape(
        target.shape + (returned.shape[2],)
    )
    summed = jnp.sum(picked.astype(jnp.float32) * gate_values[..., None], axis=2)
    return summed.astype(jnp.bfloat16)


def attend_block(query_rows, cache_rows, live_lengths, fresh_rows):
    scores = (
        jnp.einsum("nhc,nlc->nhl", query_rows, cache_rows, preferred_element_type=jnp.float32)
        * SOFTMAX_SCALE
    )
    own_score = (
        jnp.einsum("nhc,nc->nh", query_rows, fresh_rows, preferred_element_type=jnp.float32)
        * SOFTMAX_SCALE
    )
    positions = jnp.arange(cache_rows.shape[1], dtype=jnp.int32)
    scores = jnp.where(positions[None, None, :] < live_lengths[:, None, None], scores, -jnp.inf)
    row_top = jnp.maximum(jnp.max(scores, axis=2), own_score)
    weights = jnp.exp(scores - row_top[:, :, None])
    own_weight = jnp.exp(own_score - row_top)
    summed = jnp.sum(weights, axis=2) + own_weight
    blended = jnp.einsum(
        "nhl,nlc->nhc",
        weights.astype(jnp.bfloat16),
        cache_rows[:, :, :LATENT],
        preferred_element_type=jnp.float32,
    )
    own_rounded = lax.optimization_barrier(own_weight.astype(jnp.bfloat16))
    blended = blended + own_rounded.astype(jnp.float32)[:, :, None] * fresh_rows[
        :, None, :LATENT
    ].astype(jnp.float32)
    return (blended / summed[:, :, None]).astype(jnp.bfloat16)


def per_device(
    hidden,
    routes,
    route_weights,
    expert_in,
    expert_out,
    queries,
    fresh_key,
    latent_cache,
    lengths,
    swapped,
):
    n_ep = lax.axis_size("ep")
    expert_count = lax.axis_size("dp") * n_ep
    packs = [
        pack_rows(hidden[step : step + 1], routes[step : step + 1], expert_count, CAP)
        for step in range(STEPS)
    ]
    parts = 4
    tiled_pack = pack_rows_tiled(hidden[0], routes[0], expert_count, CAP, parts)
    packs[0] = tiled_pack
    received = [lax.all_to_all(p[0], ("dp", "ep"), 0, 0, tiled=True) for p in packs]
    received[0] = received[0].reshape(expert_count, CAP, hidden.shape[2])
    finished = [expert_rows(r, expert_in[0], expert_out[0]) for r in received]
    returned = [lax.all_to_all(f, ("dp", "ep"), 0, 0, tiled=True) for f in finished]
    mixed = jnp.concatenate(
        [gather_rows(returned[0], packs[0][1], route_weights[0:1])]
        + [unpack_rows(returned[step], packs[step][1], route_weights[step : step + 1]) for step in range(1, STEPS)]
    )
    row_count = swapped.shape[0]
    top_bit = lax.axis_size("dp").bit_length() - 2
    outgoing = jnp.argsort(1 - swapped, stable=True)[:MOVE]
    arrival = jnp.clip(jnp.cumsum(swapped) - 1, 0, MOVE - 1)
    is_moved = swapped == 1
    device_rows = lax.axis_index(("dp", "ep")) * row_count + jnp.arange(row_count, dtype=jnp.int32)
    total_rows = expert_count * row_count
    anchor = jnp.where(is_moved, (device_rows + total_rows // 2) % total_rows, device_rows)
    incoming_cache = swapped_2(latent_cache[outgoing], "dp", top_bit)
    merged_cache = jnp.where(is_moved[:, None, None], incoming_cache[arrival], latent_cache)
    context = attend_block(queries, merged_cache, lengths[anchor], fresh_key)
    return (mixed, context)


def solution(mesh):
    in_specs = (
        P(None, ("dp", "ep"), None),
        P(None, ("dp", "ep"), None),
        P(None, ("dp", "ep"), None),
        P(("dp", "ep"), None, None),
        P(("dp", "ep"), None, None),
        P(("dp", "ep"), None, None),
        P(("dp", "ep"), None),
        P(("dp", "ep"), None, None),
        P(),
        P(("dp", "ep")),
    )
    out_specs = (P(None, ("dp", "ep"), None), P(("dp", "ep"), None, None))
    return jax.shard_map(
        per_device, mesh=mesh, in_specs=in_specs, out_specs=out_specs, check_vma=False
    )
```

```python
import functools

import jax
import jax.numpy as jnp
from jax import lax
from jax.experimental import pallas as pl
from jax.experimental.pallas import tpu as pltpu
from jax.sharding import PartitionSpec as P

LATENT = 512
STEPS = 2
MOVE = 4
CAP = 2
MESH_ID = pl.DeviceIdType.MESH

SOFTMAX_SCALE = 192.0 ** (-0.5)


def _a2a_kernel(n_ep, n_all, x_ref, o_ref, send_sem, recv_sem):
    me = lax.axis_index("dp") * n_ep + lax.axis_index("ep")
    barrier = pltpu.get_barrier_semaphore()

    def greet(k, carry):
        peer = lax.rem(me + k, n_all)
        pl.semaphore_signal(
            barrier, 1, device_id=(peer // n_ep, peer % n_ep), device_id_type=MESH_ID
        )
        return carry

    lax.fori_loop(1, n_all, greet, 0)
    pl.semaphore_wait(barrier, n_all - 1)
    pltpu.make_async_copy(x_ref.at[me], o_ref.at[me], recv_sem).start()

    def send(k, carry):
        peer = lax.rem(me + k, n_all)
        pltpu.make_async_remote_copy(
            x_ref.at[peer],
            o_ref.at[me],
            send_sem,
            recv_sem,
            device_id=(peer // n_ep, peer % n_ep),
            device_id_type=MESH_ID,
        ).start()
        return carry

    lax.fori_loop(1, n_all, send, 0)
    sent = pl.ds(0, n_all - 1)
    pltpu.make_async_copy(x_ref.at[sent], x_ref.at[sent], send_sem).wait()
    pltpu.make_async_copy(o_ref, o_ref, recv_sem).wait()


def all_to_all_rows(x, n_ep, n_all, collective_id):
    nbytes = x.size * x.dtype.itemsize
    return pl.pallas_call(
        functools.partial(_a2a_kernel, n_ep, n_all),
        out_shape=jax.ShapeDtypeStruct(x.shape, x.dtype),
        in_specs=[pl.BlockSpec(memory_space=pl.ANY)],
        out_specs=pl.BlockSpec(memory_space=pl.ANY),
        scratch_shapes=[pltpu.SemaphoreType.DMA(()), pltpu.SemaphoreType.DMA(())],
        compiler_params=pltpu.CompilerParams(collective_id=collective_id, has_side_effects=True),
        cost_estimate=pl.CostEstimate(flops=0, transcendentals=0, bytes_accessed=2 * nbytes),
    )(x)


def swapped_2(value, axis, apart):
    mask = 2**apart
    pairs = [(source, source ^ mask) for source in range(lax.axis_size(axis))]
    return lax.ppermute(value, axis, pairs)


def expert_rows(picked, expert_in, expert_out):
    projected = jnp.einsum("skc,cf->skf", picked, expert_in, preferred_element_type=jnp.float32)
    half_width = projected.shape[2] // 2
    activated = (
        jax.nn.silu(projected[:, :, :half_width]) * projected[:, :, half_width:]
    ).astype(jnp.bfloat16)
    return jnp.einsum(
        "skf,fc->skc", activated, expert_out, preferred_element_type=jnp.float32
    ).astype(jnp.bfloat16)


def pack_rows(tokens, experts, expert_count, slot_cap):
    step_count, token_count, pick_count = experts.shape
    onehot = (experts[:, :, :, None] == jnp.arange(expert_count, dtype=jnp.int32)).astype(
        jnp.int32
    )
    flat = onehot.reshape(step_count, token_count * pick_count, expert_count)
    earlier = jnp.cumsum(flat, axis=1) - flat
    within = jnp.sum(earlier * flat, axis=2).reshape(step_count, token_count, pick_count)
    steps = jnp.arange(step_count, dtype=jnp.int32)[:, None, None]
    target = experts * (step_count * slot_cap) + steps * slot_cap + within
    places = jnp.arange(expert_count * step_count * slot_cap, dtype=jnp.int32).reshape(
        expert_count, step_count * slot_cap
    )
    flat_target = target.reshape(step_count * token_count, pick_count)
    select = jnp.any(flat_target[None, None, :, :] == places[:, :, None, None], axis=3).astype(
        jnp.bfloat16
    )
    flat_tokens = tokens.reshape(step_count * token_count, tokens.shape[2])
    packed = jnp.einsum(
        "dkt,tc->dkc", select, flat_tokens, preferred_element_type=jnp.float32
    ).astype(jnp.bfloat16)
    return packed, target


def unpack_rows(returned, target, gate_values):
    expert_count, slot_cap, _ = returned.shape
    places = jnp.arange(expert_count * slot_cap, dtype=jnp.int32).reshape(expert_count, slot_cap)
    chosen = target[..., None, None] == places
    weights = jnp.sum(jnp.where(chosen, gate_values[..., None, None], 0.0), axis=2)
    summed = jnp.einsum(
        "stek,ekc->stc",
        weights,
        returned.astype(jnp.float32),
        precision=lax.Precision.HIGHEST,
        preferred_element_type=jnp.float32,
    )
    return summed.astype(jnp.bfloat16)


def gather_rows(returned, target, gate_values):
    width = returned.shape[1]
    flat_target = target.reshape(-1)
    picked = returned[flat_target // width, flat_target % width].reshape(
        target.shape + (returned.shape[2],)
    )
    summed = jnp.sum(picked.astype(jnp.float32) * gate_values[..., None], axis=2)
    return summed.astype(jnp.bfloat16)


def attend_block(query_rows, cache_rows, live_lengths, fresh_rows):
    scores = (
        jnp.einsum("nhc,nlc->nhl", query_rows, cache_rows, preferred_element_type=jnp.float32)
        * SOFTMAX_SCALE
    )
    own_score = (
        jnp.einsum("nhc,nc->nh", query_rows, fresh_rows, preferred_element_type=jnp.float32)
        * SOFTMAX_SCALE
    )
    positions = jnp.arange(cache_rows.shape[1], dtype=jnp.int32)
    scores = jnp.where(positions[None, None, :] < live_lengths[:, None, None], scores, -jnp.inf)
    row_top = jnp.maximum(jnp.max(scores, axis=2), own_score)
    weights = jnp.exp(scores - row_top[:, :, None])
    own_weight = jnp.exp(own_score - row_top)
    summed = jnp.sum(weights, axis=2) + own_weight
    blended = jnp.einsum(
        "nhl,nlc->nhc",
        weights.astype(jnp.bfloat16),
        cache_rows[:, :, :LATENT],
        preferred_element_type=jnp.float32,
    )
    own_rounded = lax.optimization_barrier(own_weight.astype(jnp.bfloat16))
    blended = blended + own_rounded.astype(jnp.float32)[:, :, None] * fresh_rows[
        :, None, :LATENT
    ].astype(jnp.float32)
    return (blended / summed[:, :, None]).astype(jnp.bfloat16)


def per_device(
    hidden,
    routes,
    route_weights,
    expert_in,
    expert_out,
    queries,
    fresh_key,
    latent_cache,
    lengths,
    swapped,
):
    n_ep = lax.axis_size("ep")
    expert_count = lax.axis_size("dp") * n_ep
    packs = [
        pack_rows(hidden[step : step + 1], routes[step : step + 1], expert_count, CAP)
        for step in range(STEPS)
    ]
    received = [lax.all_to_all(p[0], ("dp", "ep"), 0, 0, tiled=True) for p in packs]
    finished = [expert_rows(r, expert_in[0], expert_out[0]) for r in received]
    returned = [lax.all_to_all(f, ("dp", "ep"), 0, 0, tiled=True) for f in finished]
    mixed = jnp.concatenate(
        [gather_rows(returned[0], packs[0][1], route_weights[0:1])]
        + [unpack_rows(returned[step], packs[step][1], route_weights[step : step + 1]) for step in range(1, STEPS)]
    )
    row_count = swapped.shape[0]
    top_bit = lax.axis_size("dp").bit_length() - 2
    rank = jnp.cumsum(swapped) - 1
    picks = (swapped[None, :] == 1) & (rank[None, :] == jnp.arange(MOVE, dtype=jnp.int32)[:, None])
    outgoing = jnp.sum(jnp.where(picks, jnp.arange(row_count, dtype=jnp.int32)[None, :], 0), axis=1)
    arrival = jnp.clip(jnp.cumsum(swapped) - 1, 0, MOVE - 1)
    is_moved = swapped == 1
    device_rows = lax.axis_index(("dp", "ep")) * row_count + jnp.arange(row_count, dtype=jnp.int32)
    total_rows = expert_count * row_count
    anchor = jnp.where(is_moved, (device_rows + total_rows // 2) % total_rows, device_rows)
    incoming_cache = swapped_2(latent_cache[outgoing], "dp", top_bit)
    merged_cache = jnp.where(is_moved[:, None, None], incoming_cache[arrival], latent_cache)
    context = attend_block(queries, merged_cache, lengths[anchor], fresh_key)
    return (mixed, context)


def solution(mesh):
    in_specs = (
        P(None, ("dp", "ep"), None),
        P(None, ("dp", "ep"), None),
        P(None, ("dp", "ep"), None),
        P(("dp", "ep"), None, None),
        P(("dp", "ep"), None, None),
        P(("dp", "ep"), None, None),
        P(("dp", "ep"), None),
        P(("dp", "ep"), None, None),
        P(),
        P(("dp", "ep")),
    )
    out_specs = (P(None, ("dp", "ep"), None), P(("dp", "ep"), None, None))
    return jax.shard_map(
        per_device, mesh=mesh, in_specs=in_specs, out_specs=out_specs, check_vma=False
    )
```

```python
import functools

import jax
import jax.numpy as jnp
from jax import lax
from jax.experimental import pallas as pl
from jax.experimental.pallas import tpu as pltpu
from jax.sharding import PartitionSpec as P

LATENT = 512
STEPS = 2
MOVE = 4
CAP = 2
MESH_ID = pl.DeviceIdType.MESH

SOFTMAX_SCALE = 192.0 ** (-0.5)


def _a2a_kernel(n_ep, n_all, x_ref, o_ref, send_sem, recv_sem):
    me = lax.axis_index("dp") * n_ep + lax.axis_index("ep")
    barrier = pltpu.get_barrier_semaphore()

    def greet(k, carry):
        peer = lax.rem(me + k, n_all)
        pl.semaphore_signal(
            barrier, 1, device_id=(peer // n_ep, peer % n_ep), device_id_type=MESH_ID
        )
        return carry

    lax.fori_loop(1, n_all, greet, 0)
    pl.semaphore_wait(barrier, n_all - 1)
    pltpu.make_async_copy(x_ref.at[me], o_ref.at[me], recv_sem).start()

    def send(k, carry):
        peer = lax.rem(me + k, n_all)
        pltpu.make_async_remote_copy(
            x_ref.at[peer],
            o_ref.at[me],
            send_sem,
            recv_sem,
            device_id=(peer // n_ep, peer % n_ep),
            device_id_type=MESH_ID,
        ).start()
        return carry

    lax.fori_loop(1, n_all, send, 0)
    sent = pl.ds(0, n_all - 1)
    pltpu.make_async_copy(x_ref.at[sent], x_ref.at[sent], send_sem).wait()
    pltpu.make_async_copy(o_ref, o_ref, recv_sem).wait()


def all_to_all_rows(x, n_ep, n_all, collective_id):
    nbytes = x.size * x.dtype.itemsize
    return pl.pallas_call(
        functools.partial(_a2a_kernel, n_ep, n_all),
        out_shape=jax.ShapeDtypeStruct(x.shape, x.dtype),
        in_specs=[pl.BlockSpec(memory_space=pl.ANY)],
        out_specs=pl.BlockSpec(memory_space=pl.ANY),
        scratch_shapes=[pltpu.SemaphoreType.DMA(()), pltpu.SemaphoreType.DMA(())],
        compiler_params=pltpu.CompilerParams(collective_id=collective_id, has_side_effects=True),
        cost_estimate=pl.CostEstimate(flops=0, transcendentals=0, bytes_accessed=2 * nbytes),
    )(x)


def swapped_2(value, axis, apart):
    mask = 2**apart
    pairs = [(source, source ^ mask) for source in range(lax.axis_size(axis))]
    return lax.ppermute(value, axis, pairs)


def expert_rows(picked, expert_in, expert_out):
    projected = jnp.einsum("skc,cf->skf", picked, expert_in, preferred_element_type=jnp.float32)
    half_width = projected.shape[2] // 2
    activated = (
        jax.nn.silu(projected[:, :, :half_width]) * projected[:, :, half_width:]
    ).astype(jnp.bfloat16)
    return jnp.einsum(
        "skf,fc->skc", activated, expert_out, preferred_element_type=jnp.float32
    ).astype(jnp.bfloat16)


def pack_rows(tokens, experts, expert_count, slot_cap):
    step_count, token_count, pick_count = experts.shape
    onehot = (experts[:, :, :, None] == jnp.arange(expert_count, dtype=jnp.int32)).astype(
        jnp.int32
    )
    flat = onehot.reshape(step_count, token_count * pick_count, expert_count)
    earlier = jnp.cumsum(flat, axis=1) - flat
    within = jnp.sum(earlier * flat, axis=2).reshape(step_count, token_count, pick_count)
    steps = jnp.arange(step_count, dtype=jnp.int32)[:, None, None]
    target = experts * (step_count * slot_cap) + steps * slot_cap + within
    places = jnp.arange(expert_count * step_count * slot_cap, dtype=jnp.int32).reshape(
        expert_count, step_count * slot_cap
    )
    flat_target = target.reshape(step_count * token_count, pick_count)
    select = jnp.any(flat_target[None, None, :, :] == places[:, :, None, None], axis=3).astype(
        jnp.bfloat16
    )
    flat_tokens = tokens.reshape(step_count * token_count, tokens.shape[2])
    packed = jnp.einsum(
        "dkt,tc->dkc", select, flat_tokens, preferred_element_type=jnp.float32
    ).astype(jnp.bfloat16)
    return packed, target


def unpack_rows(returned, target, gate_values, base):
    expert_count, slot_cap, _ = returned.shape
    places = jnp.arange(expert_count * slot_cap, dtype=jnp.int32).reshape(expert_count, slot_cap)
    chosen = target[..., None, None] == places
    weights = jnp.sum(jnp.where(chosen, gate_values[..., None, None], 0.0), axis=2)
    summed = jnp.einsum(
        "stek,ekc->stc",
        weights,
        returned.astype(jnp.float32),
        precision=lax.Precision.HIGHEST,
        preferred_element_type=jnp.float32,
    )
    return (summed + base).astype(jnp.bfloat16)


def gather_rows(returned, target, gate_values):
    width = returned.shape[1]
    flat_target = target.reshape(-1)
    picked = returned[flat_target // width, flat_target % width].reshape(
        target.shape + (returned.shape[2],)
    )
    summed = jnp.sum(picked.astype(jnp.float32) * gate_values[..., None], axis=2)
    return summed.astype(jnp.bfloat16)


def attend_block(query_rows, cache_rows, live_lengths, fresh_rows):
    scores = (
        jnp.einsum("nhc,nlc->nhl", query_rows, cache_rows, preferred_element_type=jnp.float32)
        * SOFTMAX_SCALE
    )
    own_score = (
        jnp.einsum("nhc,nc->nh", query_rows, fresh_rows, preferred_element_type=jnp.float32)
        * SOFTMAX_SCALE
    )
    positions = jnp.arange(cache_rows.shape[1], dtype=jnp.int32)
    scores = jnp.where(positions[None, None, :] < live_lengths[:, None, None], scores, -jnp.inf)
    row_top = jnp.maximum(jnp.max(scores, axis=2), own_score)
    weights = jnp.exp(scores - row_top[:, :, None])
    own_weight = jnp.exp(own_score - row_top)
    summed = jnp.sum(weights, axis=2) + own_weight
    blended = jnp.einsum(
        "nhl,nlc->nhc",
        weights.astype(jnp.bfloat16),
        cache_rows[:, :, :LATENT],
        preferred_element_type=jnp.float32,
    )
    own_rounded = lax.optimization_barrier(own_weight.astype(jnp.bfloat16))
    blended = blended + own_rounded.astype(jnp.float32)[:, :, None] * fresh_rows[
        :, None, :LATENT
    ].astype(jnp.float32)
    return (blended / summed[:, :, None]).astype(jnp.bfloat16)


def per_device(
    hidden,
    routes,
    route_weights,
    expert_in,
    expert_out,
    queries,
    fresh_key,
    latent_cache,
    lengths,
    swapped,
):
    n_ep = lax.axis_size("ep")
    expert_count = lax.axis_size("dp") * n_ep
    packs = [
        pack_rows(hidden[step : step + 1], routes[step : step + 1], expert_count, CAP)
        for step in range(STEPS)
    ]
    received = [lax.all_to_all(p[0], ("dp", "ep"), 0, 0, tiled=True) for p in packs]
    finished = [expert_rows(r, expert_in[0], expert_out[0]) for r in received]
    returned = [lax.all_to_all(f, ("dp", "ep"), 0, 0, tiled=True) for f in finished]
    early = gather_rows(returned[0], packs[0][1], route_weights[0:1])
    late_target = jnp.concatenate([jnp.zeros_like(packs[1][1]), packs[1][1]])
    late_gates = jnp.concatenate([jnp.zeros_like(route_weights[0:1]), route_weights[1:2]])
    earlier_rows = jnp.concatenate([early, jnp.zeros_like(early)]).astype(jnp.float32)
    mixed = unpack_rows(returned[1], late_target, late_gates, earlier_rows)
    row_count = swapped.shape[0]
    top_bit = lax.axis_size("dp").bit_length() - 2
    rank = jnp.cumsum(swapped) - 1
    picks = (swapped[None, :] == 1) & (rank[None, :] == jnp.arange(MOVE, dtype=jnp.int32)[:, None])
    outgoing = jnp.sum(jnp.where(picks, jnp.arange(row_count, dtype=jnp.int32)[None, :], 0), axis=1)
    arrival = jnp.clip(jnp.cumsum(swapped) - 1, 0, MOVE - 1)
    is_moved = swapped == 1
    device_rows = lax.axis_index(("dp", "ep")) * row_count + jnp.arange(row_count, dtype=jnp.int32)
    total_rows = expert_count * row_count
    anchor = jnp.where(is_moved, (device_rows + total_rows // 2) % total_rows, device_rows)
    incoming_cache = swapped_2(latent_cache[outgoing], "dp", top_bit)
    merged_cache = jnp.where(is_moved[:, None, None], incoming_cache[arrival], latent_cache)
    context = attend_block(queries, merged_cache, lengths[anchor], fresh_key)
    return (mixed, context)


def solution(mesh):
    in_specs = (
        P(None, ("dp", "ep"), None),
        P(None, ("dp", "ep"), None),
        P(None, ("dp", "ep"), None),
        P(("dp", "ep"), None, None),
        P(("dp", "ep"), None, None),
        P(("dp", "ep"), None, None),
        P(("dp", "ep"), None),
        P(("dp", "ep"), None, None),
        P(),
        P(("dp", "ep")),
    )
    out_specs = (P(None, ("dp", "ep"), None), P(("dp", "ep"), None, None))
    return jax.shard_map(
        per_device, mesh=mesh, in_specs=in_specs, out_specs=out_specs, check_vma=False
    )
```

```python
import functools

import jax
import jax.numpy as jnp
from jax import lax
from jax.experimental import pallas as pl
from jax.experimental.pallas import tpu as pltpu
from jax.sharding import PartitionSpec as P

LATENT = 512
STEPS = 2
MOVE = 4
CAP = 2
MESH_ID = pl.DeviceIdType.MESH

SOFTMAX_SCALE = 192.0 ** (-0.5)


def _a2a_kernel(n_ep, n_all, x_ref, o_ref, send_sem, recv_sem):
    me = lax.axis_index("dp") * n_ep + lax.axis_index("ep")
    barrier = pltpu.get_barrier_semaphore()

    def greet(k, carry):
        peer = lax.rem(me + k, n_all)
        pl.semaphore_signal(
            barrier, 1, device_id=(peer // n_ep, peer % n_ep), device_id_type=MESH_ID
        )
        return carry

    lax.fori_loop(1, n_all, greet, 0)
    pl.semaphore_wait(barrier, n_all - 1)
    pltpu.make_async_copy(x_ref.at[me], o_ref.at[me], recv_sem).start()

    def send(k, carry):
        peer = lax.rem(me + k, n_all)
        pltpu.make_async_remote_copy(
            x_ref.at[peer],
            o_ref.at[me],
            send_sem,
            recv_sem,
            device_id=(peer // n_ep, peer % n_ep),
            device_id_type=MESH_ID,
        ).start()
        return carry

    lax.fori_loop(1, n_all, send, 0)
    sent = pl.ds(0, n_all - 1)
    pltpu.make_async_copy(x_ref.at[sent], x_ref.at[sent], send_sem).wait()
    pltpu.make_async_copy(o_ref, o_ref, recv_sem).wait()


def all_to_all_rows(x, n_ep, n_all, collective_id):
    nbytes = x.size * x.dtype.itemsize
    return pl.pallas_call(
        functools.partial(_a2a_kernel, n_ep, n_all),
        out_shape=jax.ShapeDtypeStruct(x.shape, x.dtype),
        in_specs=[pl.BlockSpec(memory_space=pl.ANY)],
        out_specs=pl.BlockSpec(memory_space=pl.ANY),
        scratch_shapes=[pltpu.SemaphoreType.DMA(()), pltpu.SemaphoreType.DMA(())],
        compiler_params=pltpu.CompilerParams(collective_id=collective_id, has_side_effects=True),
        cost_estimate=pl.CostEstimate(flops=0, transcendentals=0, bytes_accessed=2 * nbytes),
    )(x)


def swapped_2(value, axis, apart):
    mask = 2**apart
    pairs = [(source, source ^ mask) for source in range(lax.axis_size(axis))]
    return lax.ppermute(value, axis, pairs)


def expert_rows(picked, expert_in, expert_out):
    projected = jnp.einsum("skc,cf->skf", picked, expert_in, preferred_element_type=jnp.float32)
    half_width = projected.shape[2] // 2
    activated = (
        jax.nn.silu(projected[:, :, :half_width]) * projected[:, :, half_width:]
    ).astype(jnp.bfloat16)
    return jnp.einsum(
        "skf,fc->skc", activated, expert_out, preferred_element_type=jnp.float32
    ).astype(jnp.bfloat16)


def pack_rows(tokens, experts, expert_count, slot_cap):
    step_count, token_count, pick_count = experts.shape
    onehot = (experts[:, :, :, None] == jnp.arange(expert_count, dtype=jnp.int32)).astype(
        jnp.int32
    )
    flat = onehot.reshape(step_count, token_count * pick_count, expert_count)
    earlier = jnp.cumsum(flat, axis=1) - flat
    within = jnp.sum(earlier * flat, axis=2).reshape(step_count, token_count, pick_count)
    steps = jnp.arange(step_count, dtype=jnp.int32)[:, None, None]
    target = experts * (step_count * slot_cap) + steps * slot_cap + within
    places = jnp.arange(expert_count * step_count * slot_cap, dtype=jnp.int32).reshape(
        expert_count, step_count * slot_cap
    )
    flat_target = target.reshape(step_count * token_count, pick_count)
    select = jnp.any(flat_target[None, None, :, :] == places[:, :, None, None], axis=3).astype(
        jnp.bfloat16
    )
    flat_tokens = tokens.reshape(step_count * token_count, tokens.shape[2])
    packed = jnp.einsum(
        "dkt,tc->dkc", select, flat_tokens, preferred_element_type=jnp.float32
    ).astype(jnp.bfloat16)
    return packed, target


def unpack_rows(returned, target, gate_values, base):
    expert_count, slot_cap, _ = returned.shape
    places = jnp.arange(expert_count * slot_cap, dtype=jnp.int32).reshape(expert_count, slot_cap)
    chosen = target[..., None, None] == places
    weights = jnp.sum(jnp.where(chosen, gate_values[..., None, None], 0.0), axis=2)
    summed = jnp.einsum(
        "stek,ekc->stc",
        weights,
        returned.astype(jnp.float32),
        precision=lax.Precision.HIGH,
        preferred_element_type=jnp.float32,
    )
    return (summed + base).astype(jnp.bfloat16)


def gather_rows(returned, target, gate_values):
    width = returned.shape[1]
    flat_target = target.reshape(-1)
    picked = returned[flat_target // width, flat_target % width].reshape(
        target.shape + (returned.shape[2],)
    )
    summed = jnp.sum(picked.astype(jnp.float32) * gate_values[..., None], axis=2)
    return summed.astype(jnp.bfloat16)


def attend_block(query_rows, cache_rows, live_lengths, fresh_rows):
    scores = (
        jnp.einsum("nhc,nlc->nhl", query_rows, cache_rows, preferred_element_type=jnp.float32)
        * SOFTMAX_SCALE
    )
    own_score = (
        jnp.einsum("nhc,nc->nh", query_rows, fresh_rows, preferred_element_type=jnp.float32)
        * SOFTMAX_SCALE
    )
    positions = jnp.arange(cache_rows.shape[1], dtype=jnp.int32)
    scores = jnp.where(positions[None, None, :] < live_lengths[:, None, None], scores, -jnp.inf)
    row_top = jnp.maximum(jnp.max(scores, axis=2), own_score)
    weights = jnp.exp(scores - row_top[:, :, None])
    own_weight = jnp.exp(own_score - row_top)
    summed = jnp.sum(weights, axis=2) + own_weight
    blended = jnp.einsum(
        "nhl,nlc->nhc",
        weights.astype(jnp.bfloat16),
        cache_rows[:, :, :LATENT],
        preferred_element_type=jnp.float32,
    )
    own_rounded = lax.optimization_barrier(own_weight.astype(jnp.bfloat16))
    blended = blended + own_rounded.astype(jnp.float32)[:, :, None] * fresh_rows[
        :, None, :LATENT
    ].astype(jnp.float32)
    return (blended / summed[:, :, None]).astype(jnp.bfloat16)


def per_device(
    hidden,
    routes,
    route_weights,
    expert_in,
    expert_out,
    queries,
    fresh_key,
    latent_cache,
    lengths,
    swapped,
):
    n_ep = lax.axis_size("ep")
    expert_count = lax.axis_size("dp") * n_ep
    packs = [
        pack_rows(hidden[step : step + 1], routes[step : step + 1], expert_count, CAP)
        for step in range(STEPS)
    ]
    received = [lax.all_to_all(p[0], ("dp", "ep"), 0, 0, tiled=True) for p in packs]
    finished = [expert_rows(r, expert_in[0], expert_out[0]) for r in received]
    returned = [lax.all_to_all(f, ("dp", "ep"), 0, 0, tiled=True) for f in finished]
    early = gather_rows(returned[0], packs[0][1], route_weights[0:1])
    late_target = jnp.concatenate([jnp.zeros_like(packs[1][1]), packs[1][1]])
    late_gates = jnp.concatenate([jnp.zeros_like(route_weights[0:1]), route_weights[1:2]])
    earlier_rows = jnp.concatenate([early, jnp.zeros_like(early)]).astype(jnp.float32)
    mixed = unpack_rows(returned[1], late_target, late_gates, earlier_rows)
    row_count = swapped.shape[0]
    top_bit = lax.axis_size("dp").bit_length() - 2
    rank = jnp.cumsum(swapped) - 1
    picks = (swapped[None, :] == 1) & (rank[None, :] == jnp.arange(MOVE, dtype=jnp.int32)[:, None])
    outgoing = jnp.sum(jnp.where(picks, jnp.arange(row_count, dtype=jnp.int32)[None, :], 0), axis=1)
    arrival = jnp.clip(jnp.cumsum(swapped) - 1, 0, MOVE - 1)
    is_moved = swapped == 1
    device_rows = lax.axis_index(("dp", "ep")) * row_count + jnp.arange(row_count, dtype=jnp.int32)
    total_rows = expert_count * row_count
    anchor = jnp.where(is_moved, (device_rows + total_rows // 2) % total_rows, device_rows)
    incoming_cache = swapped_2(latent_cache[outgoing], "dp", top_bit)
    merged_cache = jnp.where(is_moved[:, None, None], incoming_cache[arrival], latent_cache)
    context = attend_block(queries, merged_cache, lengths[anchor], fresh_key)
    return (mixed, context)


def solution(mesh):
    in_specs = (
        P(None, ("dp", "ep"), None),
        P(None, ("dp", "ep"), None),
        P(None, ("dp", "ep"), None),
        P(("dp", "ep"), None, None),
        P(("dp", "ep"), None, None),
        P(("dp", "ep"), None, None),
        P(("dp", "ep"), None),
        P(("dp", "ep"), None, None),
        P(),
        P(("dp", "ep")),
    )
    out_specs = (P(None, ("dp", "ep"), None), P(("dp", "ep"), None, None))
    return jax.shard_map(
        per_device, mesh=mesh, in_specs=in_specs, out_specs=out_specs, check_vma=False
    )
```

```python
import functools

import jax
import jax.numpy as jnp
from jax import lax
from jax.experimental import pallas as pl
from jax.experimental.pallas import tpu as pltpu
from jax.sharding import PartitionSpec as P

LATENT = 512
STEPS = 2
MOVE = 4
CAP = 2
MESH_ID = pl.DeviceIdType.MESH

SOFTMAX_SCALE = 192.0 ** (-0.5)


def _a2a_kernel(n_ep, n_all, x_ref, o_ref, send_sem, recv_sem):
    me = lax.axis_index("dp") * n_ep + lax.axis_index("ep")
    barrier = pltpu.get_barrier_semaphore()

    def greet(k, carry):
        peer = lax.rem(me + k, n_all)
        pl.semaphore_signal(
            barrier, 1, device_id=(peer // n_ep, peer % n_ep), device_id_type=MESH_ID
        )
        return carry

    lax.fori_loop(1, n_all, greet, 0)
    pl.semaphore_wait(barrier, n_all - 1)
    pltpu.make_async_copy(x_ref.at[me], o_ref.at[me], recv_sem).start()

    def send(k, carry):
        peer = lax.rem(me + k, n_all)
        pltpu.make_async_remote_copy(
            x_ref.at[peer],
            o_ref.at[me],
            send_sem,
            recv_sem,
            device_id=(peer // n_ep, peer % n_ep),
            device_id_type=MESH_ID,
        ).start()
        return carry

    lax.fori_loop(1, n_all, send, 0)
    sent = pl.ds(0, n_all - 1)
    pltpu.make_async_copy(x_ref.at[sent], x_ref.at[sent], send_sem).wait()
    pltpu.make_async_copy(o_ref, o_ref, recv_sem).wait()


def all_to_all_rows(x, n_ep, n_all, collective_id):
    nbytes = x.size * x.dtype.itemsize
    return pl.pallas_call(
        functools.partial(_a2a_kernel, n_ep, n_all),
        out_shape=jax.ShapeDtypeStruct(x.shape, x.dtype),
        in_specs=[pl.BlockSpec(memory_space=pl.ANY)],
        out_specs=pl.BlockSpec(memory_space=pl.ANY),
        scratch_shapes=[pltpu.SemaphoreType.DMA(()), pltpu.SemaphoreType.DMA(())],
        compiler_params=pltpu.CompilerParams(collective_id=collective_id, has_side_effects=True),
        cost_estimate=pl.CostEstimate(flops=0, transcendentals=0, bytes_accessed=2 * nbytes),
    )(x)


def swapped_2(value, axis, apart):
    mask = 2**apart
    pairs = [(source, source ^ mask) for source in range(lax.axis_size(axis))]
    return lax.ppermute(value, axis, pairs)


def expert_rows(picked, expert_in, expert_out):
    projected = jnp.einsum("skc,cf->skf", picked, expert_in, preferred_element_type=jnp.float32)
    half_width = projected.shape[2] // 2
    activated = (
        jax.nn.silu(projected[:, :, :half_width]) * projected[:, :, half_width:]
    ).astype(jnp.bfloat16)
    return jnp.einsum(
        "skf,fc->skc", activated, expert_out, preferred_element_type=jnp.float32
    ).astype(jnp.bfloat16)


def pack_rows(tokens, experts, expert_count, slot_cap):
    step_count, token_count, pick_count = experts.shape
    onehot = (experts[:, :, :, None] == jnp.arange(expert_count, dtype=jnp.int32)).astype(
        jnp.int32
    )
    flat = onehot.reshape(step_count, token_count * pick_count, expert_count)
    earlier = jnp.cumsum(flat, axis=1) - flat
    within = jnp.sum(earlier * flat, axis=2).reshape(step_count, token_count, pick_count)
    steps = jnp.arange(step_count, dtype=jnp.int32)[:, None, None]
    target = experts * (step_count * slot_cap) + steps * slot_cap + within
    places = jnp.arange(expert_count * step_count * slot_cap, dtype=jnp.int32).reshape(
        expert_count, step_count * slot_cap
    )
    flat_target = target.reshape(step_count * token_count, pick_count)
    select = jnp.any(flat_target[None, None, :, :] == places[:, :, None, None], axis=3).astype(
        jnp.bfloat16
    )
    flat_tokens = tokens.reshape(step_count * token_count, tokens.shape[2])
    packed = jnp.einsum(
        "dkt,tc->dkc", select, flat_tokens, preferred_element_type=jnp.float32
    ).astype(jnp.bfloat16)
    return packed, target


def pack_rows_tiled(tokens, experts, expert_count, slot_cap, parts):
    token_count, pick_count = experts.shape
    onehot = (experts[:, :, None] == jnp.arange(expert_count, dtype=jnp.int32)).astype(jnp.int32)
    flat = onehot.reshape(token_count * pick_count, expert_count)
    earlier = jnp.cumsum(flat, axis=0) - flat
    within = jnp.sum(earlier * flat, axis=1).reshape(token_count, pick_count)
    target = experts * slot_cap + within
    slots = jnp.arange(expert_count * slot_cap, dtype=jnp.int32)
    hit = jnp.any(target[None, :, :] == slots[:, None, None], axis=2).astype(jnp.bfloat16)
    eye = jnp.eye(parts, dtype=jnp.bfloat16)
    select = (hit[:, None, :, None] * eye[None, :, None, :]).reshape(
        expert_count * slot_cap * parts, token_count * parts
    )
    pieces = tokens.reshape(token_count * parts, tokens.shape[1] // parts)
    packed = jnp.dot(
        select,
        pieces,
        preferred_element_type=jnp.float32,
    ).astype(jnp.bfloat16)
    return packed.reshape(expert_count, slot_cap * parts, pieces.shape[1]), target[None]


def unpack_rows(returned, target, gate_values, base):
    expert_count, slot_cap, _ = returned.shape
    places = jnp.arange(expert_count * slot_cap, dtype=jnp.int32).reshape(expert_count, slot_cap)
    chosen = target[..., None, None] == places
    weights = jnp.sum(jnp.where(chosen, gate_values[..., None, None], 0.0), axis=2)
    summed = jnp.einsum(
        "stek,ekc->stc",
        weights,
        returned.astype(jnp.float32),
        precision=lax.Precision.HIGHEST,
        preferred_element_type=jnp.float32,
    )
    return (summed + base).astype(jnp.bfloat16)


def gather_rows(returned, target, gate_values):
    width = returned.shape[1]
    flat_target = target.reshape(-1)
    picked = returned[flat_target // width, flat_target % width].reshape(
        target.shape + (returned.shape[2],)
    )
    summed = jnp.sum(picked.astype(jnp.float32) * gate_values[..., None], axis=2)
    return summed.astype(jnp.bfloat16)


def attend_block(query_rows, cache_rows, live_lengths, fresh_rows):
    scores = (
        jnp.einsum("nhc,nlc->nhl", query_rows, cache_rows, preferred_element_type=jnp.float32)
        * SOFTMAX_SCALE
    )
    own_score = (
        jnp.einsum("nhc,nc->nh", query_rows, fresh_rows, preferred_element_type=jnp.float32)
        * SOFTMAX_SCALE
    )
    positions = jnp.arange(cache_rows.shape[1], dtype=jnp.int32)
    scores = jnp.where(positions[None, None, :] < live_lengths[:, None, None], scores, -jnp.inf)
    row_top = jnp.maximum(jnp.max(scores, axis=2), own_score)
    weights = jnp.exp(scores - row_top[:, :, None])
    own_weight = jnp.exp(own_score - row_top)
    summed = jnp.sum(weights, axis=2) + own_weight
    blended = jnp.einsum(
        "nhl,nlc->nhc",
        weights.astype(jnp.bfloat16),
        cache_rows[:, :, :LATENT],
        preferred_element_type=jnp.float32,
    )
    own_rounded = lax.optimization_barrier(own_weight.astype(jnp.bfloat16))
    blended = blended + own_rounded.astype(jnp.float32)[:, :, None] * fresh_rows[
        :, None, :LATENT
    ].astype(jnp.float32)
    return (blended / summed[:, :, None]).astype(jnp.bfloat16)


def per_device(
    hidden,
    routes,
    route_weights,
    expert_in,
    expert_out,
    queries,
    fresh_key,
    latent_cache,
    lengths,
    swapped,
):
    n_ep = lax.axis_size("ep")
    expert_count = lax.axis_size("dp") * n_ep
    packs = [
        pack_rows(hidden[step : step + 1], routes[step : step + 1], expert_count, CAP)
        for step in range(STEPS)
    ]
    parts = 4
    tiled_pack = pack_rows_tiled(hidden[0], routes[0], expert_count, CAP, parts)
    packs[0] = tiled_pack
    received = [lax.all_to_all(p[0], ("dp", "ep"), 0, 0, tiled=True) for p in packs]
    received[0] = received[0].reshape(expert_count, CAP, hidden.shape[2])
    finished = [expert_rows(r, expert_in[0], expert_out[0]) for r in received]
    returned = [lax.all_to_all(f, ("dp", "ep"), 0, 0, tiled=True) for f in finished]
    early = gather_rows(returned[0], packs[0][1], route_weights[0:1])
    late_target = jnp.concatenate([jnp.zeros_like(packs[1][1]), packs[1][1]])
    late_gates = jnp.concatenate([jnp.zeros_like(route_weights[0:1]), route_weights[1:2]])
    earlier_rows = jnp.concatenate([early, jnp.zeros_like(early)]).astype(jnp.float32)
    mixed = unpack_rows(returned[1], late_target, late_gates, earlier_rows)
    row_count = swapped.shape[0]
    top_bit = lax.axis_size("dp").bit_length() - 2
    rank = jnp.cumsum(swapped) - 1
    picks = (swapped[None, :] == 1) & (rank[None, :] == jnp.arange(MOVE, dtype=jnp.int32)[:, None])
    outgoing = jnp.sum(jnp.where(picks, jnp.arange(row_count, dtype=jnp.int32)[None, :], 0), axis=1)
    arrival = jnp.clip(jnp.cumsum(swapped) - 1, 0, MOVE - 1)
    is_moved = swapped == 1
    device_rows = lax.axis_index(("dp", "ep")) * row_count + jnp.arange(row_count, dtype=jnp.int32)
    total_rows = expert_count * row_count
    anchor = jnp.where(is_moved, (device_rows + total_rows // 2) % total_rows, device_rows)
    incoming_cache = swapped_2(latent_cache[outgoing], "dp", top_bit)
    merged_cache = jnp.where(is_moved[:, None, None], incoming_cache[arrival], latent_cache)
    context = attend_block(queries, merged_cache, lengths[anchor], fresh_key)
    return (mixed, context)


def solution(mesh):
    in_specs = (
        P(None, ("dp", "ep"), None),
        P(None, ("dp", "ep"), None),
        P(None, ("dp", "ep"), None),
        P(("dp", "ep"), None, None),
        P(("dp", "ep"), None, None),
        P(("dp", "ep"), None, None),
        P(("dp", "ep"), None),
        P(("dp", "ep"), None, None),
        P(),
        P(("dp", "ep")),
    )
    out_specs = (P(None, ("dp", "ep"), None), P(("dp", "ep"), None, None))
    return jax.shard_map(
        per_device, mesh=mesh, in_specs=in_specs, out_specs=out_specs, check_vma=False
    )
```
